256 devices in a mesh: row: 32 (over z_hi, x, core), col: 8 (over y, z_lo).
Axes of the slice: x: 4, y: 4, z: 8 (z_hi: 4, z_lo: 2; z = z_hi * 2 + z_lo), core: 2. Of those that a mesh axis runs over, the one named last changes fastest.
Arguments:
- amplitudes: float32 [2, 32, 8, 262144], P(None, 'row', 'col'), may hold values from -6 to 6
- gate_matrices: float32 [5, 4, 2, 128, 128], replicated, may hold values from -0.375 to 0.375
- permutation: int32 [32], replicated, may hold values from 0 to 31, each once
Outputs:
- evolved: float32 [2, 32, 8, 262144], P(None, 'row', 'col')
The draws below stay inside these ranges and needn't reach their ends.
Inputs may be any that keep to these rules, and one draw needn't show every extreme that they name: `permutation`: each value from 0 to 31 appears once.
All inputs are finite; a program needn't handle non-finite values.
Results may differ from the reference program's by a relative error of at most 0.00014.
Values sent between devices are 32-bit elements; how exact they have to be, the bound alone decides.
No kernel may reach another device: no remote copies, remote signals or barrier semaphores. Data moves between devices by JAX's collectives and lax.ppermute only.
A program may use at most 64 MiB of HBM per device.

```python
import jax
import jax.numpy as jnp
from jax import lax

GD = 128
AMP_DEV = 262144
SEGS = 5
GATES = 4
N_ROW = 32
N_COL = 8


def shard_levels(own_key, shape, shards, smallest, top_value):
    level = 1.0
    for position, shards_of in shards:
        heights = jax.random.uniform(jax.random.fold_in(jax.random.fold_in(own_key, 6), position), (shards_of,), jnp.float32, smallest / len(shards), top_value / len(shards))
        level = level * jnp.repeat(jnp.exp(heights), shape[position] // shards_of).reshape((-1,) + (1,) * (len(shape) - 1 - position))
    return level


def noise(key, shape, scale, bound, cuts=(), dtype=jnp.bfloat16):
    values = scale * jax.random.normal(key, shape, jnp.float32)
    if cuts:
        values = values * shard_levels(key, shape, cuts, -0.22, 0.18)
    return jnp.clip(values, -bound, bound).astype(dtype)


def setup_inputs(seed: int = 0) -> dict:
    keys = jax.random.split(jax.random.key(seed), 4)
    return {
        "amplitudes": noise(keys[0], (2, N_ROW, N_COL, AMP_DEV), 1.0, 6.0, ((1, 32), (2, 8)), jnp.float32),
        "gate_matrices": noise(keys[1], (SEGS, GATES, 2, GD, GD), (2 * GD) ** -0.5, 0.375, (), jnp.float32),
        "permutation": jax.random.permutation(keys[2], N_ROW).astype(jnp.int32),
    }


HIGHEST = lax.Precision.HIGHEST
GATE_KINDS = ("top", "mid", "low", "top")


def stacked(gate_mat):
    real_part = gate_mat[0]
    imag_part = gate_mat[1]
    top_rows = jnp.concatenate([real_part, -imag_part], axis=1)
    bottom_rows = jnp.concatenate([imag_part, real_part], axis=1)
    return jnp.concatenate([top_rows, bottom_rows], axis=0)


def gate_whole(field, gate_mat, kind):
    gate_size = gate_mat.shape[-1]
    real_quad = stacked(gate_mat).reshape(2, gate_size, 2, gate_size)
    groups = field.shape[1]
    amp_count = field.shape[2]
    if kind == "top":
        shaped = field.reshape(2, groups, gate_size, amp_count // gate_size)
        result = jnp.einsum("djck,cpkm->dpjm", real_quad, shaped, precision=HIGHEST)
    elif kind == "mid":
        shaped = field.reshape(2, groups, amp_count // (gate_size * gate_size), gate_size, gate_size)
        result = jnp.einsum("djck,cpakb->dpajb", real_quad, shaped, precision=HIGHEST)
    else:
        shaped = field.reshape(2, groups, amp_count // gate_size, gate_size)
        result = jnp.einsum("djck,cpmk->dpmj", real_quad, shaped, precision=HIGHEST)
    return result.reshape(2, groups, amp_count)


def segment(field, seg_mats):
    full_shape = field.shape
    flat_field = field.reshape(2, N_ROW * N_COL, AMP_DEV)
    for number in range(seg_mats.shape[0]):
        flat_field = gate_whole(flat_field, seg_mats[number], GATE_KINDS[number])
    return flat_field.reshape(full_shape)


def swap_row_bit(field, bit_pos):
    stride = 2 ** bit_pos
    shaped = field.reshape(2, N_ROW // (2 * stride), 2, stride, N_COL, 2, AMP_DEV // 2)
    return jnp.swapaxes(shaped, 2, 5).reshape(2, N_ROW, N_COL, AMP_DEV)


def swap_col_top(field):
    shaped = field.reshape(2, N_ROW, 2, N_COL // 2, 2, AMP_DEV // 2)
    return jnp.swapaxes(shaped, 2, 4).reshape(2, N_ROW, N_COL, AMP_DEV)


def reference(amplitudes, gate_matrices, permutation):
    row_bits = int(N_ROW).bit_length() - 1
    field = segment(amplitudes, gate_matrices[0])
    field = swap_row_bit(field, 0)
    field = segment(field, gate_matrices[1])
    field = swap_row_bit(field, row_bits - 1)
    field = segment(field, gate_matrices[2])
    shaped = field.reshape(2, N_ROW, N_COL, N_ROW, AMP_DEV // N_ROW)
    shaped = jnp.swapaxes(shaped, 1, 3)
    shaped = shaped[:, :, :, permutation, :]
    field = shaped.reshape(2, N_ROW, N_COL, AMP_DEV)
    field = segment(field, gate_matrices[3])
    field = swap_col_top(field)
    return segment(field, gate_matrices[4])
```

```python
import functools

import jax
import jax.numpy as jnp
from jax import lax
from jax.experimental import pallas as pl
from jax.experimental.pallas import tpu as pltpu
from jax.sharding import PartitionSpec as P


HIGHEST = lax.Precision.HIGHEST
F32 = jnp.float32
BF16 = jnp.bfloat16
GD = 128
HALF = 64
LIMIT = 16 << 20
STATE = (16, 16, 8, 128)
PART = (8, 16, 8, 128)


def split(value):
    high = value.astype(BF16)
    return high, (value - high.astype(F32)).astype(BF16)


def onehot(kind, ids_ref, perm_ref):
    new = lax.broadcasted_iota(jnp.int32, (GD, GD), 0)
    old = lax.broadcasted_iota(jnp.int32, (GD, GD), 1)
    z_own, x_own, c_own = ids_ref[0], ids_ref[1], ids_ref[2]
    rest, core, block = new & 3, (new >> 2) & 1, new >> 3
    if kind == "mid":
        want = ((new & 7) << 4) | (new >> 3)
    elif kind[:3] == "xor":
        want = new ^ (ids_ref[int(kind[3:])] << 6)
    elif kind == "dest":
        x = ((block >> 2) + x_own) & 3
        z = ((block & 3) + z_own) & 3
        want = (((((z << 2) | x) << 1) | (core ^ c_own)) << 2) | rest
    else:
        z = (z_own - (block >> 2)) & 3
        x = (x_own - (block & 3)) & 3
        want = (((((z << 2) | x) << 1) | (core ^ c_own)) << 2) | rest
        old = jnp.broadcast_to(perm_ref[...], (GD, GD))
    return jnp.where(want == old, 1.0, 0.0).astype(BF16)


def weight_kernel(kinds, ids_ref, gates_ref, perm_ref, out_ref):
    made = {}
    for number, (rows, cols) in enumerate(kinds):
        for kind in (rows, cols):
            if kind is not None and kind not in made:
                made[kind] = onehot(kind, ids_ref, perm_ref)
        slot = (0, 1, 3)[number]
        real_high, real_low = split(gates_ref[0, slot, 0])
        imag_high, imag_low = split(gates_ref[0, slot, 1])
        wide = jnp.concatenate([real_high, imag_high, real_low, imag_low], axis=1)
        if rows is not None:
            wide = jnp.dot(made[rows], wide, preferred_element_type=F32).astype(BF16)
        parts = [wide[:, GD * i : GD * (i + 1)] for i in range(4)]
        if cols is not None:
            tall = lax.dot_general(
                jnp.concatenate(parts, axis=0),
                made[cols],
                (((1,), (1,)), ((), ())),
                preferred_element_type=F32,
            ).astype(BF16)
            parts = [tall[GD * i : GD * (i + 1)] for i in range(4)]
        out_ref[number, 0:GD, 0:GD] = parts[0]
        out_ref[number, 0:GD, GD:] = parts[1]
        out_ref[number, GD:, 0:GD] = parts[2]
        out_ref[number, GD:, GD:] = parts[3]


def weights(gate_matrices, seg, kinds, ids, perm_row):
    return pl.pallas_call(
        functools.partial(weight_kernel, kinds),
        out_shape=jax.ShapeDtypeStruct((3, 256, 256), BF16),
        grid_spec=pltpu.PrefetchScalarGridSpec(
            num_scalar_prefetch=1,
            grid=(1,),
            in_specs=[
                pl.BlockSpec((1, 4, 2, GD, GD), lambda i, ids: (seg, 0, 0, 0, 0)),
                pl.BlockSpec((1, GD), lambda i, ids: (0, 0)),
            ],
            out_specs=pl.BlockSpec((3, 256, 256), lambda i, ids: (0, 0, 0)),
        ),
        cost_estimate=pl.CostEstimate(
            flops=3 * 2 * 640 * 128 * 512, bytes_accessed=1 << 20, transcendentals=0
        ),
    )(ids, gate_matrices, perm_row)


def gate_step(first, second, w_high_low, w_high, sign):
    state = jnp.concatenate([first, second], axis=1)
    turned = jnp.concatenate(
        [pltpu.roll(first, HALF, 1) * sign, pltpu.roll(second, HALF, 1) * sign], axis=1
    )
    high, low = split(jnp.concatenate([state, turned], axis=0))
    both = jnp.dot(w_high_low, high, preferred_element_type=F32)
    small = jnp.dot(w_high, low, preferred_element_type=F32)
    return both[:GD] + (both[GD:] + small)


def segment_kernel(source, target, n_in, n_after, *refs):
    w_ref = refs[0]
    ins = refs[1 : 1 + n_in]
    outs = refs[1 + n_in + n_after : -2]
    one, two = refs[-2:]
    lane = lax.broadcasted_iota(jnp.int32, (1, GD), 1)
    sign = jnp.where(lane < HALF, -1.0, 1.0)
    upper = lax.broadcasted_iota(jnp.int32, (1, 8, GD), 1) >= 4

    def load_start(i):
        blocks = []
        for p in (2 * i, 2 * i + 1):
            re = ins[0][0, pl.ds(p, GD, stride=16), :]
            im = ins[0][1, pl.ds(p, GD, stride=16), :]
            if source[1] == 0:
                blocks.append(jnp.where(lane < HALF, re, pltpu.roll(im, HALF, 1)))
            else:
                blocks.append(jnp.where(lane < HALF, pltpu.roll(re, HALF, 1), im))
        return blocks

    def load_pair(i):
        return [
            jnp.concatenate(
                [ins[0][:, p].reshape(HALF, GD), ins[1][:, p].reshape(HALF, GD)], axis=0
            )
            for p in (2 * i, 2 * i + 1)
        ]

    def load_remap(i):
        near = jnp.concatenate([ref[:, 0, i] for ref in ins[:4]], axis=0)
        far = jnp.concatenate([ref[:, 1, i] for ref in ins[:4]], axis=0)
        even = jnp.where(upper, pltpu.roll(far, 4, 1), near)
        odd = jnp.where(upper, far, pltpu.roll(near, 4, 1))
        return [even.reshape(GD, GD), odd.reshape(GD, GD)]

    load = {"start": load_start, "pair": load_pair, "remap": load_remap}[source[0]]

    def top_first(i, carry):
        first, second = load(i)
        result = gate_step(first, second, w_ref[0], w_ref[0, :GD], sign)
        one[:, 2 * i] = result[:, :GD].reshape(16, 8, GD)
        one[:, 2 * i + 1] = result[:, GD:].reshape(16, 8, GD)
        return carry

    def mid(i, carry):
        first = one[2 * i].reshape(GD, GD)
        second = one[2 * i + 1].reshape(GD, GD)
        result = gate_step(first, second, w_ref[1], w_ref[1, :GD], sign)
        two[2 * i] = result[:, :GD].reshape(16, 8, GD)
        two[2 * i + 1] = result[:, GD:].reshape(16, 8, GD)
        return carry

    def top_last(i, carry):
        first = two[:, 2 * i].reshape(GD, GD)
        second = two[:, 2 * i + 1].reshape(GD, GD)
        result = gate_step(first, second, w_ref[2], w_ref[2, :GD], sign)
        pieces = (result[:, :GD], result[:, GD:])
        if target == "pair":
            for p, piece in zip((2 * i, 2 * i + 1), pieces):
                outs[0][:, p] = piece[:HALF].reshape(8, 8, GD)
                outs[1][:, p] = piece[HALF:].reshape(8, 8, GD)
        elif target == "remap":
            even, odd = (piece.reshape(16, 8, GD) for piece in pieces)
            near = jnp.where(upper, pltpu.roll(odd, 4, 1), even)
            far = jnp.where(upper, odd, pltpu.roll(even, 4, 1))
            for x in range(4):
                outs[2 * x][:, i] = near[4 * x : 4 * x + 4]
                outs[2 * x + 1][:, i] = far[4 * x : 4 * x + 4]
        elif target == "plain":
            for p, piece in zip((2 * i, 2 * i + 1), pieces):
                outs[0][:, p] = piece.reshape(16, 8, GD)
        else:
            other_ref, low_ref = ins[n_in - 2], ins[n_in - 1]
            for p, piece in zip((2 * i, 2 * i + 1), pieces):
                rows = jnp.concatenate([other_ref[:, p].reshape(GD, GD), piece], axis=1)
                high, low = split(rows)
                done = jnp.dot(high, low_ref[0], preferred_element_type=F32) + (
                    jnp.dot(high, low_ref[1], preferred_element_type=F32)
                    + jnp.dot(low, low_ref[0], preferred_element_type=F32)
                )
                outs[0][0, pl.ds(p, GD, stride=16), :] = done[:, :GD]
                outs[0][1, pl.ds(p, GD, stride=16), :] = done[:, GD:]
        return carry

    for step in (top_first, mid, top_last):
        lax.fori_loop(0, 8, step, 0)


def run_segment(source, target, w, ins, extra=(), after=()):
    if target == "pair":
        out_shape = [jax.ShapeDtypeStruct(PART, F32)] * 2
    elif target == "remap":
        out_shape = [jax.ShapeDtypeStruct((4, 8, 8, 128), F32)] * 8
    elif target == "plain":
        out_shape = [jax.ShapeDtypeStruct(STATE, F32)]
    else:
        out_shape = [jax.ShapeDtypeStruct((2, 2048, 128), F32)]
    args = list(ins) + list(extra)
    vmem = pl.BlockSpec(memory_space=pltpu.VMEM)
    return pl.pallas_call(
        functools.partial(segment_kernel, source, target, len(args), len(after)),
        out_shape=out_shape,
        in_specs=[vmem] * (1 + len(args)) + [pl.BlockSpec(memory_space=pl.ANY)] * len(after),
        out_specs=[vmem] * len(out_shape),
        scratch_shapes=[pltpu.VMEM(STATE, F32)] * 2,
        cost_estimate=pl.CostEstimate(
            flops=3 * 3 * 2 * 128 * 256 * 2048, bytes_accessed=3 << 20, transcendentals=0
        ),
        compiler_params=pltpu.CompilerParams(vmem_limit_bytes=LIMIT),
    )(w, *args, *after)


def regroup_kernel(*refs):
    ins, outs = refs[:8], refs[8:]
    for z in range(4):
        for x in range(4):
            for c in range(2):
                outs[z][x, c] = ins[2 * x + c][z]


def regroup(blocks):
    vmem = pl.BlockSpec(memory_space=pltpu.VMEM)
    return pl.pallas_call(
        regroup_kernel,
        out_shape=[jax.ShapeDtypeStruct((4, 2, 8, 8, 128), F32)] * 4,
        in_specs=[vmem] * 8,
        out_specs=[vmem] * 4,
        cost_estimate=pl.CostEstimate(flops=0, bytes_accessed=2 << 20, transcendentals=0),
        compiler_params=pltpu.CompilerParams(vmem_limit_bytes=LIMIT),
    )(*blocks)


def flip(value, axis, mask):
    return lax.ppermute(value, axis, [(s, s ^ mask) for s in range(lax.axis_size(axis))])


def shift_row(value, z, x, c):
    pairs = []
    for s in range(32):
        to = ((((s >> 3) + z) & 3) << 3) | ((((s >> 1) + x) & 3) << 1) | ((s & 1) ^ c)
        pairs.append((s, to))
    return lax.ppermute(value, "row", pairs)


def stacked(gate_mat):
    real_part = gate_mat[0]
    imag_part = gate_mat[1]
    top_rows = jnp.concatenate([real_part, -imag_part], axis=1)
    bottom_rows = jnp.concatenate([imag_part, real_part], axis=1)
    return jnp.concatenate([top_rows, bottom_rows], axis=0)


def low_weights(gate_matrices):
    total = stacked(gate_matrices[0, 2])
    for seg in range(1, gate_matrices.shape[0]):
        total = jnp.dot(stacked(gate_matrices[seg, 2]), total, precision=HIGHEST)
    rows = total.T.reshape(2, 2, HALF, 256).transpose(1, 0, 2, 3).reshape(256, 256)
    high = lax.reduce_precision(rows, 8, 7)
    return jnp.stack([high.astype(BF16), (rows - high).astype(BF16)])


def circuit(amplitudes, gate_matrices, permutation):
    state = amplitudes.reshape(2, 2048, 128)
    row = lax.axis_index("row")
    col = lax.axis_index("col")
    ids = jnp.stack([row >> 3, (row >> 1) & 3, row & 1, row >> 4, col >> 2]).astype(jnp.int32)
    perm_row = (permutation[:, None] * 4 + jnp.arange(4, dtype=jnp.int32)).reshape(1, GD)
    mid = ("mid", "mid")
    kinds = (
        ((None, None), mid, ("xor2", None)),
        ((None, "xor2"), mid, ("xor3", None)),
        ((None, "xor3"), mid, ("dest", None)),
        ((None, "src"), mid, ("xor4", None)),
        ((None, "xor4"), mid, (None, None)),
    )
    w = [weights(gate_matrices, seg, kinds[seg], ids, perm_row) for seg in range(5)]
    low = low_weights(gate_matrices)
    halves = (0, 1)
    kept, sent = {}, {}
    after = ()
    for h in halves:
        kept[h], out = run_segment(("start", h), "pair", w[0], [state], after=after)
        after = (out,)
        sent[h] = flip(out, "row", 1)
    after = ()
    for h in halves:
        kept[h], out = run_segment(("pair",), "pair", w[1], [kept[h], sent[h]], after=after)
        after = (out,)
        sent[h] = flip(out, "row", 16)
    got = {}
    after = ()
    for h in halves:
        blocks = run_segment(("pair",), "remap", w[2], [kept[h], sent[h]], after=after)
        moved = [
            block if k == 0 else shift_row(block, 0, k >> 1, k & 1)
            for k, block in enumerate(blocks)
        ]
        groups = regroup(moved)
        after = (groups[0],)
        got[h] = [groups[0]]
        for z in range(1, 4):
            got[h].append(shift_row(groups[z], z, 0, 0))
    after = ()
    for h in halves:
        kept[h], out = run_segment(("remap",), "pair", w[3], got[h], after=after)
        after = (out,)
        sent[h] = flip(out, "col", 4)
    (first,) = run_segment(("pair",), "plain", w[4], [kept[0], sent[0]])
    (out,) = run_segment(("pair",), "low", w[4], [kept[1], sent[1]], [first, low])
    return out.reshape(amplitudes.shape)


def solution(mesh):
    placed = (P(None, "row", "col", None), P(), P())
    return jax.shard_map(
        circuit, mesh=mesh, in_specs=placed, out_specs=P(None, "row", "col", None), check_vma=False
    )
```

```python
import functools

import jax
import jax.numpy as jnp
from jax import lax
from jax.experimental import pallas as pl
from jax.experimental.pallas import tpu as pltpu
from jax.sharding import PartitionSpec as P


F32 = jnp.float32
BF16 = jnp.bfloat16
GD = 128
HALF = 64
LIMIT = 16 << 20
STATE = (16, 16, 8, 128)
PART = (8, 16, 8, 128)


def split(value):
    high = value.astype(BF16)
    return high, (value - high.astype(F32)).astype(BF16)


def onehot(kind, perm_ref):
    row = lax.axis_index("row")
    col = lax.axis_index("col")
    new = lax.broadcasted_iota(jnp.int32, (GD, GD), 0)
    old = lax.broadcasted_iota(jnp.int32, (GD, GD), 1)
    z_own, x_own, c_own = row >> 3, (row >> 1) & 3, row & 1
    rest, core, block = new & 3, (new >> 2) & 1, new >> 3
    if kind == "mid":
        want = ((new & 7) << 4) | (new >> 3)
    elif kind[:3] == "xor":
        want = new ^ ({"xor2": c_own, "xor3": row >> 4, "xor4": col >> 2}[kind] << 6)
    elif kind == "dest":
        x = ((block >> 2) + x_own) & 3
        z = ((block & 3) + z_own) & 3
        want = (((((z << 2) | x) << 1) | (core ^ c_own)) << 2) | rest
    else:
        z = (z_own - (block >> 2)) & 3
        x = (x_own - (block & 3)) & 3
        want = (((((z << 2) | x) << 1) | (core ^ c_own)) << 2) | rest
        state = lax.broadcasted_iota(jnp.int32, (1, GD), 1)
        moved = state & 3
        for t in range(32):
            moved += jnp.where(state >> 2 == t, perm_ref[t] * 4, 0)
        old = jnp.broadcast_to(moved, (GD, GD))
    return jnp.where(want == old, 1.0, 0.0).astype(BF16)


def weight_kernel(kinds, perm_ref, gates_ref, out_ref):
    made = {}
    for number, (rows, cols) in enumerate(kinds):
        for kind in (rows, cols):
            if kind is not None and kind not in made:
                made[kind] = onehot(kind, perm_ref)
        slot = (0, 1, 3)[number]
        real_high, real_low = split(gates_ref[0, slot, 0])
        imag_high, imag_low = split(gates_ref[0, slot, 1])
        wide = jnp.concatenate([real_high, imag_high, real_low, imag_low], axis=1)
        if rows is not None:
            wide = jnp.dot(made[rows], wide, preferred_element_type=F32).astype(BF16)
        parts = [wide[:, GD * i : GD * (i + 1)] for i in range(4)]
        if cols is not None:
            tall = lax.dot_general(
                jnp.concatenate(parts, axis=0),
                made[cols],
                (((1,), (1,)), ((), ())),
                preferred_element_type=F32,
            ).astype(BF16)
            parts = [tall[GD * i : GD * (i + 1)] for i in range(4)]
        out_ref[number, 0:GD, 0:GD] = parts[0]
        out_ref[number, 0:GD, GD:] = parts[1]
        out_ref[number, GD:, 0:GD] = parts[2]
        out_ref[number, GD:, GD:] = parts[3]


def weights(gate_matrices, seg, kinds, permutation):
    return pl.pallas_call(
        functools.partial(weight_kernel, kinds),
        out_shape=jax.ShapeDtypeStruct((3, 256, 256), BF16),
        grid_spec=pltpu.PrefetchScalarGridSpec(
            num_scalar_prefetch=1,
            grid=(1,),
            in_specs=[pl.BlockSpec((1, 4, 2, GD, GD), lambda i, perm: (seg, 0, 0, 0, 0))],
            out_specs=pl.BlockSpec(memory_space=pltpu.VMEM),
        ),
        cost_estimate=pl.CostEstimate(
            flops=3 * 2 * 640 * 128 * 512, bytes_accessed=1 << 20, transcendentals=0
        ),
        compiler_params=pltpu.CompilerParams(vmem_limit_bytes=LIMIT),
    )(permutation, gate_matrices)


def low_kernel(gates_ref, out_ref, total_ref):
    seg = pl.program_id(0)
    real, imag = gates_ref[0, 0, 0], gates_ref[0, 0, 1]
    form = jnp.concatenate(
        [jnp.concatenate([real, -imag], axis=1), jnp.concatenate([imag, real], axis=1)], axis=0
    )

    @pl.when(seg == 0)
    def _():
        new = lax.broadcasted_iota(jnp.int32, (256, 256), 0)
        old = lax.broadcasted_iota(jnp.int32, (256, 256), 1)
        want = (((new >> 6) & 1) << 7) | ((new >> 7) << 6) | (new & 63)
        total_ref[...] = jnp.where(want == old, 1.0, 0.0)

    high, low = split(total_ref[...])
    form_high, form_low = split(form)

    def times(left, right):
        return lax.dot_general(
            left, right, (((1,), (1,)), ((), ())), preferred_element_type=F32
        )

    total = times(high, form_high) + (times(high, form_low) + times(low, form_high))
    total_ref[...] = total
    out_ref[0], out_ref[1] = split(total)


def low_weights(gate_matrices):
    return pl.pallas_call(
        low_kernel,
        out_shape=jax.ShapeDtypeStruct((2, 256, 256), BF16),
        grid=(gate_matrices.shape[0],),
        in_specs=[pl.BlockSpec((1, 1, 2, GD, GD), lambda i: (i, 2, 0, 0, 0))],
        out_specs=pl.BlockSpec(memory_space=pltpu.VMEM),
        scratch_shapes=[pltpu.VMEM((256, 256), F32)],
        cost_estimate=pl.CostEstimate(
            flops=5 * 3 * 2 * 256**3, bytes_accessed=1 << 20, transcendentals=0
        ),
        compiler_params=pltpu.CompilerParams(vmem_limit_bytes=LIMIT),
        name="low_weights",
    )(gate_matrices)


def gate_step(first, second, w_high_low, w_high, sign):
    state = jnp.concatenate([first, second], axis=1)
    turned = jnp.concatenate(
        [pltpu.roll(first, HALF, 1) * sign, pltpu.roll(second, HALF, 1) * sign], axis=1
    )
    high, low = split(jnp.concatenate([state, turned], axis=0))
    both = jnp.dot(w_high_low, high, preferred_element_type=F32)
    small = jnp.dot(w_high, low, preferred_element_type=F32)
    return both[:GD] + (both[GD:] + small)


def segment_kernel(source, target, n_in, unroll, *refs):
    w_ref = refs[0]
    ins = refs[1 : 1 + n_in]
    outs = refs[1 + n_in : -2]
    one, two = refs[-2:]
    lane = lax.broadcasted_iota(jnp.int32, (1, GD), 1)
    sign = jnp.where(lane < HALF, -1.0, 1.0)
    upper = lax.broadcasted_iota(jnp.int32, (1, 8, GD), 1) >= 4

    def load_start(i):
        blocks = []
        for p in (2 * i, 2 * i + 1):
            re = ins[0][0, pl.ds(p, GD, stride=16), :]
            im = ins[0][1, pl.ds(p, GD, stride=16), :]
            if source[1] == 0:
                blocks.append(jnp.where(lane < HALF, re, pltpu.roll(im, HALF, 1)))
            else:
                blocks.append(jnp.where(lane < HALF, pltpu.roll(re, HALF, 1), im))
        return blocks

    def load_pair(i):
        return [
            jnp.concatenate(
                [ins[0][:, p].reshape(HALF, GD), ins[1][:, p].reshape(HALF, GD)], axis=0
            )
            for p in (2 * i, 2 * i + 1)
        ]

    def load_remap(i):
        near = jnp.concatenate([ref[:, 0, i] for ref in ins[:4]], axis=0)
        far = jnp.concatenate([ref[:, 1, i] for ref in ins[:4]], axis=0)
        even = jnp.where(upper, pltpu.roll(far, 4, 1), near)
        odd = jnp.where(upper, far, pltpu.roll(near, 4, 1))
        return [even.reshape(GD, GD), odd.reshape(GD, GD)]

    load = {"start": load_start, "pair": load_pair, "remap": load_remap}[source[0]]

    def top_first(i, carry):
        first, second = load(i)
        result = gate_step(first, second, w_ref[0], w_ref[0, :GD], sign)
        one[:, 2 * i] = result[:, :GD].reshape(16, 8, GD)
        one[:, 2 * i + 1] = result[:, GD:].reshape(16, 8, GD)
        return carry

    def mid(i, carry):
        first = one[2 * i].reshape(GD, GD)
        second = one[2 * i + 1].reshape(GD, GD)
        result = gate_step(first, second, w_ref[1], w_ref[1, :GD], sign)
        two[2 * i] = result[:, :GD].reshape(16, 8, GD)
        two[2 * i + 1] = result[:, GD:].reshape(16, 8, GD)
        return carry

    def top_last(i, carry):
        first = two[:, 2 * i].reshape(GD, GD)
        second = two[:, 2 * i + 1].reshape(GD, GD)
        result = gate_step(first, second, w_ref[2], w_ref[2, :GD], sign)
        pieces = (result[:, :GD], result[:, GD:])
        if target == "pair":
            for p, piece in zip((2 * i, 2 * i + 1), pieces):
                outs[0][:, p] = piece[:HALF].reshape(8, 8, GD)
                outs[1][:, p] = piece[HALF:].reshape(8, 8, GD)
        elif target == "remap":
            even, odd = (piece.reshape(16, 8, GD) for piece in pieces)
            near = jnp.where(upper, pltpu.roll(odd, 4, 1), even)
            far = jnp.where(upper, odd, pltpu.roll(even, 4, 1))
            for x in range(4):
                outs[2 * x][:, i] = near[4 * x : 4 * x + 4]
                outs[2 * x + 1][:, i] = far[4 * x : 4 * x + 4]
        else:
            held = outs[0] if target == "plain" else one
            for p, piece in zip((2 * i, 2 * i + 1), pieces):
                held[:, p] = piece.reshape(16, 8, GD)
        return carry

    def low_gate(i, carry):
        other_ref, low_ref = ins[n_in - 2], ins[n_in - 1]
        rows = [
            jnp.concatenate(
                [other_ref[:, p].reshape(GD, GD), one[:, p].reshape(GD, GD)], axis=1
            )
            for p in range(4 * i, 4 * i + 4)
        ]
        high, low = split(jnp.concatenate(rows, axis=0))
        done = jnp.dot(high, low_ref[0], preferred_element_type=F32) + (
            jnp.dot(high, low_ref[1], preferred_element_type=F32)
            + jnp.dot(low, low_ref[0], preferred_element_type=F32)
        )
        for k in range(4):
            piece = done[GD * k : GD * (k + 1)]
            outs[0][0, pl.ds(4 * i + k, GD, stride=16), :] = piece[:, :GD]
            outs[0][1, pl.ds(4 * i + k, GD, stride=16), :] = piece[:, GD:]
        return carry

    for step in (top_first, mid, top_last):
        lax.fori_loop(0, 8, step, 0, unroll=unroll)
    if target == "low":
        for i in range(4):
            low_gate(i, 0)


def run_segment(source, target, w, ins, extra=(), unroll=8):
    if target == "pair":
        out_shape = [jax.ShapeDtypeStruct(PART, F32)] * 2
    elif target == "remap":
        out_shape = [jax.ShapeDtypeStruct((4, 8, 8, 128), F32)] * 8
    elif target == "plain":
        out_shape = [jax.ShapeDtypeStruct(STATE, F32)]
    else:
        out_shape = [jax.ShapeDtypeStruct((2, 2048, 128), F32)]
    args = list(ins) + list(extra)
    vmem = pl.BlockSpec(memory_space=pltpu.VMEM)
    return pl.pallas_call(
        functools.partial(segment_kernel, source, target, len(args), unroll),
        out_shape=out_shape,
        in_specs=[vmem] * (1 + len(args)),
        out_specs=[vmem] * len(out_shape),
        scratch_shapes=[pltpu.VMEM(STATE, F32)] * 2,
        cost_estimate=pl.CostEstimate(
            flops=3 * 3 * 2 * 128 * 256 * 2048, bytes_accessed=3 << 20, transcendentals=0
        ),
        compiler_params=pltpu.CompilerParams(vmem_limit_bytes=LIMIT),
    )(w, *args)


def regroup_kernel(*refs):
    ins, outs = refs[:8], refs[8:]
    for z in range(4):
        for x in range(4):
            for c in range(2):
                outs[z][x, c] = ins[2 * x + c][z]


def regroup(blocks):
    vmem = pl.BlockSpec(memory_space=pltpu.VMEM)
    return pl.pallas_call(
        regroup_kernel,
        out_shape=[jax.ShapeDtypeStruct((4, 2, 8, 8, 128), F32)] * 4,
        in_specs=[vmem] * 8,
        out_specs=[vmem] * 4,
        cost_estimate=pl.CostEstimate(flops=0, bytes_accessed=2 << 20, transcendentals=0),
        compiler_params=pltpu.CompilerParams(vmem_limit_bytes=LIMIT),
    )(*blocks)


def flip(value, axis, mask):
    return lax.ppermute(value, axis, [(s, s ^ mask) for s in range(lax.axis_size(axis))])


def shift_row(value, z, x, c):
    pairs = []
    for s in range(32):
        to = ((((s >> 3) + z) & 3) << 3) | ((((s >> 1) + x) & 3) << 1) | ((s & 1) ^ c)
        pairs.append((s, to))
    return lax.ppermute(value, "row", pairs)


def circuit(amplitudes, gate_matrices, permutation):
    state = amplitudes.reshape(2, 2048, 128)
    mid = ("mid", "mid")
    kinds = (
        ((None, None), mid, ("xor2", None)),
        ((None, "xor2"), mid, ("xor3", None)),
        ((None, "xor3"), mid, ("dest", None)),
        ((None, "src"), mid, ("xor4", None)),
        ((None, "xor4"), mid, (None, None)),
    )
    w = [weights(gate_matrices, seg, kinds[seg], permutation) for seg in range(5)]
    low = low_weights(gate_matrices)
    halves = (0, 1)
    kept, sent = {}, {}
    for h in halves:
        kept[h], out = run_segment(("start", h), "pair", w[0], [state])
        sent[h] = flip(out, "row", 1)
    for h in halves:
        kept[h], out = run_segment(("pair",), "pair", w[1], [kept[h], sent[h]], unroll=(8, 4)[h])
        sent[h] = flip(out, "row", 16)
    got = {}
    for h in halves:
        blocks = run_segment(("pair",), "remap", w[2], [kept[h], sent[h]], unroll=(8, 4)[h])
        moved = [
            block if k == 0 else shift_row(block, 0, k >> 1, k & 1)
            for k, block in enumerate(blocks)
        ]
        groups = regroup(moved)
        got[h] = [groups[0]]
        for z in range(1, 4):
            got[h].append(shift_row(groups[z], z, 0, 0))
    for h in halves:
        kept[h], out = run_segment(("remap",), "pair", w[3], got[h], unroll=(4, 8)[h])
        sent[h] = flip(out, "col", 4)
    (first,) = run_segment(("pair",), "plain", w[4], [kept[0], sent[0]], unroll=4)
    (out,) = run_segment(("pair",), "low", w[4], [kept[1], sent[1]], [first, low])
    return out.reshape(amplitudes.shape)


def solution(mesh):
    placed = (P(None, "row", "col", None), P(), P())
    return jax.shard_map(
        circuit, mesh=mesh, in_specs=placed, out_specs=P(None, "row", "col", None), check_vma=False
    )
```

```python
import functools

import jax
import jax.numpy as jnp
from jax import lax
from jax.experimental import pallas as pl
from jax.experimental.pallas import tpu as pltpu
from jax.sharding import PartitionSpec as P


F32 = jnp.float32
BF16 = jnp.bfloat16
GD = 128
HALF = 64
LIMIT = 16 << 20
STATE = (16, 16, 8, 128)
PART = (8, 16, 8, 128)


def split(value):
    high = value.astype(BF16)
    return high, (value - high.astype(F32)).astype(BF16)


def onehot(kind, perm_ref):
    row = lax.axis_index("row")
    col = lax.axis_index("col")
    new = lax.broadcasted_iota(jnp.int32, (GD, GD), 0)
    old = lax.broadcasted_iota(jnp.int32, (GD, GD), 1)
    z_own, x_own, c_own = row >> 3, (row >> 1) & 3, row & 1
    rest, core, block = new & 3, (new >> 2) & 1, new >> 3
    if kind == "mid":
        want = ((new & 7) << 4) | (new >> 3)
    elif kind[:3] == "xor":
        want = new ^ ({"xor2": c_own, "xor3": row >> 4, "xor4": col >> 2}[kind] << 6)
    elif kind == "dest":
        x = ((block >> 2) + x_own) & 3
        z = ((block & 3) + z_own) & 3
        want = (((((z << 2) | x) << 1) | (core ^ c_own)) << 2) | rest
    else:
        z = (z_own - (block >> 2)) & 3
        x = (x_own - (block & 3)) & 3
        want = (((((z << 2) | x) << 1) | (core ^ c_own)) << 2) | rest
        state = lax.broadcasted_iota(jnp.int32, (1, GD), 1)
        moved = state & 3
        for t in range(32):
            moved += jnp.where(state >> 2 == t, perm_ref[t] * 4, 0)
        old = jnp.broadcast_to(moved, (GD, GD))
    return jnp.where(want == old, 1.0, 0.0).astype(BF16)


def weight_kernel(kinds, *refs):
    perm_ref = refs[0] if len(refs) == 3 else None
    gates_ref, out_ref = refs[-2:]
    made = {}
    for number, (rows, cols) in enumerate(kinds):
        for kind in (rows, cols):
            if kind is not None and kind not in made:
                made[kind] = onehot(kind, perm_ref)
        slot = (0, 1, 3)[number]
        real_high, real_low = split(gates_ref[0, slot, 0])
        imag_high, imag_low = split(gates_ref[0, slot, 1])
        wide = jnp.concatenate([real_high, imag_high, real_low, imag_low], axis=1)
        if rows is not None:
            wide = jnp.dot(made[rows], wide, preferred_element_type=F32).astype(BF16)
        parts = [wide[:, GD * i : GD * (i + 1)] for i in range(4)]
        if cols is not None:
            tall = lax.dot_general(
                jnp.concatenate(parts, axis=0),
                made[cols],
                (((1,), (1,)), ((), ())),
                preferred_element_type=F32,
            ).astype(BF16)
            parts = [tall[GD * i : GD * (i + 1)] for i in range(4)]
        out_ref[number, 0:GD, 0:GD] = parts[0]
        out_ref[number, 0:GD, GD:] = parts[1]
        out_ref[number, GD:, 0:GD] = parts[2]
        out_ref[number, GD:, GD:] = parts[3]


def weights(gate_matrices, seg, kinds, permutation):
    prefetch = () if permutation is None else (permutation,)
    block = seg
    if seg == 0:
        block, gate_matrices = 0, gate_matrices[:1]
    return pl.pallas_call(
        functools.partial(weight_kernel, kinds),
        out_shape=jax.ShapeDtypeStruct((3, 256, 256), BF16),
        grid_spec=pltpu.PrefetchScalarGridSpec(
            num_scalar_prefetch=len(prefetch),
            grid=(1,),
            in_specs=[pl.BlockSpec((1, 4, 2, GD, GD), lambda i, *_: (block, 0, 0, 0, 0))],
            out_specs=pl.BlockSpec(memory_space=pltpu.VMEM),
        ),
        cost_estimate=pl.CostEstimate(
            flops=3 * 2 * 640 * 128 * 512, bytes_accessed=1 << 20, transcendentals=0
        ),
        compiler_params=pltpu.CompilerParams(vmem_limit_bytes=LIMIT),
    )(*prefetch, gate_matrices)


def low_kernel(gates_ref, out_ref, total_ref):
    seg = pl.program_id(0)
    real, imag = gates_ref[0, 0, 0], gates_ref[0, 0, 1]
    form = jnp.concatenate(
        [jnp.concatenate([real, -imag], axis=1), jnp.concatenate([imag, real], axis=1)], axis=0
    )

    @pl.when(seg == 0)
    def _():
        new = lax.broadcasted_iota(jnp.int32, (256, 256), 0)
        old = lax.broadcasted_iota(jnp.int32, (256, 256), 1)
        want = (((new >> 6) & 1) << 7) | ((new >> 7) << 6) | (new & 63)
        total_ref[...] = jnp.where(want == old, 1.0, 0.0)

    high, low = split(total_ref[...])
    form_high, form_low = split(form)

    def times(left, right):
        return lax.dot_general(
            left, right, (((1,), (1,)), ((), ())), preferred_element_type=F32
        )

    total = times(high, form_high) + (times(high, form_low) + times(low, form_high))
    total_ref[...] = total
    for k, piece in enumerate(split(total)):
        for h in range(2):
            rows = piece[GD * h : GD * (h + 1)]
            out_ref[h, k, 0:GD] = rows
            out_ref[h, k, GD:] = rows


def low_weights(gate_matrices):
    return pl.pallas_call(
        low_kernel,
        out_shape=jax.ShapeDtypeStruct((2, 2, 256, 256), BF16),
        grid=(gate_matrices.shape[0],),
        in_specs=[pl.BlockSpec((1, 1, 2, GD, GD), lambda i: (i, 2, 0, 0, 0))],
        out_specs=pl.BlockSpec(memory_space=pltpu.VMEM),
        scratch_shapes=[pltpu.VMEM((256, 256), F32)],
        cost_estimate=pl.CostEstimate(
            flops=5 * 3 * 2 * 256**3, bytes_accessed=1 << 20, transcendentals=0
        ),
        compiler_params=pltpu.CompilerParams(vmem_limit_bytes=LIMIT),
        name="low_weights",
    )(gate_matrices)


def gate_step(first, second, w_high_low, w_high, sign):
    state = jnp.concatenate([first, second], axis=1)
    turned = jnp.concatenate(
        [pltpu.roll(first, HALF, 1) * sign, pltpu.roll(second, HALF, 1) * sign], axis=1
    )
    high, low = split(jnp.concatenate([state, turned], axis=0))
    both = jnp.dot(w_high_low, high, preferred_element_type=F32)
    small = jnp.dot(w_high, low, preferred_element_type=F32)
    return both[:GD] + (both[GD:] + small)


def segment_kernel(source, target, n_in, unroll, *refs):
    w_ref = refs[0]
    ins = refs[1 : 1 + n_in]
    outs = refs[1 + n_in : -2]
    one, two = refs[-2:]
    lane = lax.broadcasted_iota(jnp.int32, (1, GD), 1)
    sign = jnp.where(lane < HALF, -1.0, 1.0)
    upper = lax.broadcasted_iota(jnp.int32, (1, 8, GD), 1) >= 4

    def load_start(i):
        blocks = []
        for p in (2 * i, 2 * i + 1):
            re = ins[0][0, pl.ds(p, GD, stride=16), :]
            im = ins[0][1, pl.ds(p, GD, stride=16), :]
            if source[1] == 0:
                blocks.append(jnp.where(lane < HALF, re, pltpu.roll(im, HALF, 1)))
            else:
                blocks.append(jnp.where(lane < HALF, pltpu.roll(re, HALF, 1), im))
        return blocks

    def load_pair(i):
        return [
            jnp.concatenate(
                [ins[0][:, p].reshape(HALF, GD), ins[1][:, p].reshape(HALF, GD)], axis=0
            )
            for p in (2 * i, 2 * i + 1)
        ]

    def load_remap(i):
        def half(c):
            if source[1] == "by_x":
                blocks = [ins[x][z, c, i] for z in range(4) for x in range(4)]
                return jnp.stack(blocks, axis=0)
            return jnp.concatenate([ins[2 * z + c][:, i] for z in range(4)], axis=0)

        near, far = half(0), half(1)
        even = jnp.where(upper, pltpu.roll(far, 4, 1), near)
        odd = jnp.where(upper, far, pltpu.roll(near, 4, 1))
        return [even.reshape(GD, GD), odd.reshape(GD, GD)]

    load = {"start": load_start, "pair": load_pair, "remap": load_remap}[source[0]]

    def top_first(i, carry):
        first, second = load(i)
        result = gate_step(first, second, w_ref[0], w_ref[0, :GD], sign)
        one[:, 2 * i] = result[:, :GD].reshape(16, 8, GD)
        one[:, 2 * i + 1] = result[:, GD:].reshape(16, 8, GD)
        return carry

    def mid(i, carry):
        first = one[2 * i].reshape(GD, GD)
        second = one[2 * i + 1].reshape(GD, GD)
        result = gate_step(first, second, w_ref[1], w_ref[1, :GD], sign)
        two[2 * i] = result[:, :GD].reshape(16, 8, GD)
        two[2 * i + 1] = result[:, GD:].reshape(16, 8, GD)
        return carry

    def top_last(i, carry):
        first = two[:, 2 * i].reshape(GD, GD)
        second = two[:, 2 * i + 1].reshape(GD, GD)
        result = gate_step(first, second, w_ref[2], w_ref[2, :GD], sign)
        pieces = (result[:, :GD], result[:, GD:])
        if target == "pair":
            for p, piece in zip((2 * i, 2 * i + 1), pieces):
                outs[0][:, p] = piece[:HALF].reshape(8, 8, GD)
                outs[1][:, p] = piece[HALF:].reshape(8, 8, GD)
        elif target in ("by_x", "by_z"):
            even, odd = (piece.reshape(16, 8, GD) for piece in pieces)
            near = jnp.where(upper, pltpu.roll(odd, 4, 1), even)
            far = jnp.where(upper, odd, pltpu.roll(even, 4, 1))
            for x in range(4):
                if target == "by_x":
                    outs[x][:, 0, i] = near[4 * x : 4 * x + 4]
                    outs[x][:, 1, i] = far[4 * x : 4 * x + 4]
                    continue
                for z in range(4):
                    outs[2 * z][x, i] = near[4 * x + z]
                    outs[2 * z + 1][x, i] = far[4 * x + z]
        else:
            for p, piece in zip((2 * i, 2 * i + 1), pieces):
                one[:, p] = piece.reshape(16, 8, GD)
        return carry

    def low_gate(i, carry):
        low_ref = ins[-1]
        rows = jnp.concatenate([one[:, 4 * i + k].reshape(GD, GD) for k in range(4)], axis=0)
        pair = jnp.concatenate(split(rows), axis=1)
        done = jnp.dot(pair, low_ref[source[1], 0], preferred_element_type=F32) + jnp.dot(
            pair, low_ref[source[1], 1], preferred_element_type=F32
        )
        if target == "share":
            outs[0][i] = done
            return carry
        done = done + ins[-2][i]
        for k in range(4):
            piece = done[GD * k : GD * (k + 1)]
            outs[0][0, pl.ds(4 * i + k, GD, stride=16), :] = piece[:, :GD]
            outs[0][1, pl.ds(4 * i + k, GD, stride=16), :] = piece[:, GD:]
        return carry

    for step in (top_first, mid, top_last):
        lax.fori_loop(0, 8, step, 0, unroll=unroll)
    if target in ("share", "low"):
        lax.fori_loop(0, 4, low_gate, 0, unroll=4 if unroll == 8 else 1)


def run_segment(source, target, w, ins, extra=(), unroll=8):
    if target == "pair":
        out_shape = [jax.ShapeDtypeStruct(PART, F32)] * 2
    elif target == "by_x":
        out_shape = [jax.ShapeDtypeStruct((4, 2, 8, 8, 128), F32)] * 4
    elif target == "by_z":
        out_shape = [jax.ShapeDtypeStruct((4, 8, 8, 128), F32)] * 8
    elif target == "share":
        out_shape = [jax.ShapeDtypeStruct((4, 512, 256), F32)]
    else:
        out_shape = [jax.ShapeDtypeStruct((2, 2048, 128), F32)]
    args = list(ins) + list(extra)
    vmem = pl.BlockSpec(memory_space=pltpu.VMEM)
    return pl.pallas_call(
        functools.partial(segment_kernel, source, target, len(args), unroll),
        out_shape=out_shape,
        in_specs=[vmem] * (1 + len(args)),
        out_specs=[vmem] * len(out_shape),
        scratch_shapes=[pltpu.VMEM(STATE, F32)] * 2,
        cost_estimate=pl.CostEstimate(
            flops=3 * 3 * 2 * 128 * 256 * 2048, bytes_accessed=3 << 20, transcendentals=0
        ),
        compiler_params=pltpu.CompilerParams(vmem_limit_bytes=LIMIT),
    )(w, *args)


def regroup_kernel(target, *refs):
    by_z, by_x = (refs[:8], refs[8:]) if target == "by_x" else (refs[4:], refs[:4])
    for z in range(4):
        for x in range(4):
            for c in range(2):
                if target == "by_x":
                    by_x[x][z, c] = by_z[2 * z + c][x]
                else:
                    by_z[2 * z + c][x] = by_x[x][z, c]


def regroup(target, blocks):
    vmem = pl.BlockSpec(memory_space=pltpu.VMEM)
    by_x = [jax.ShapeDtypeStruct((4, 2, 8, 8, 128), F32)] * 4
    by_z = [jax.ShapeDtypeStruct((4, 8, 8, 128), F32)] * 8
    out_shape = by_x if target == "by_x" else by_z
    return pl.pallas_call(
        functools.partial(regroup_kernel, target),
        out_shape=out_shape,
        in_specs=[vmem] * len(blocks),
        out_specs=[vmem] * len(out_shape),
        cost_estimate=pl.CostEstimate(flops=0, bytes_accessed=2 << 20, transcendentals=0),
        compiler_params=pltpu.CompilerParams(vmem_limit_bytes=LIMIT),
    )(*blocks)


def flip(value, axis, mask):
    return lax.ppermute(value, axis, [(s, s ^ mask) for s in range(lax.axis_size(axis))])


def shift_row(value, z, x, c):
    pairs = []
    for s in range(32):
        to = ((((s >> 3) + z) & 3) << 3) | ((((s >> 1) + x) & 3) << 1) | ((s & 1) ^ c)
        pairs.append((s, to))
    return lax.ppermute(value, "row", pairs)


def shift_x(blocks):
    moved = [blocks[0]]
    for x in range(1, 4):
        moved.append(shift_row(blocks[x], 0, x, 0))
    return moved


def shift_z(blocks):
    moved = [blocks[0]]
    for k in range(1, 8):
        moved.append(shift_row(blocks[k], k >> 1, 0, k & 1))
    return moved


def circuit(amplitudes, gate_matrices, permutation):
    state = amplitudes.reshape(2, 2048, 128)
    mid = ("mid", "mid")
    kinds = (
        ((None, None), mid, ("xor2", None)),
        ((None, "xor2"), mid, ("xor3", None)),
        ((None, "xor3"), mid, ("dest", None)),
        ((None, "src"), mid, ("xor4", None)),
        ((None, "xor4"), mid, (None, None)),
    )
    w = [
        weights(gate_matrices, seg, kinds[seg], permutation if seg == 3 else None)
        for seg in range(5)
    ]
    low = low_weights(gate_matrices)
    halves = (0, 1)
    kept, sent = {}, {}
    for h in halves:
        kept[h], out = run_segment(("start", h), "pair", w[0], [state])
        sent[h] = flip(out, "row", 1)
    for h in halves:
        kept[h], out = run_segment(("pair",), "pair", w[1], [kept[h], sent[h]], unroll=(8, 4)[h])
        sent[h] = flip(out, "row", 16)
    got = {}
    blocks = run_segment(("pair",), "by_z", w[2], [kept[0], sent[0]])
    got[0] = shift_x(regroup("by_x", shift_z(blocks)))
    blocks = run_segment(("pair",), "by_x", w[2], [kept[1], sent[1]])
    got[1] = shift_z(regroup("by_z", shift_x(blocks)))
    for h in halves:
        kept[h], out = run_segment(
            ("remap", ("by_x", "by_z")[h]), "pair", w[3], got[h], unroll=(4, 8)[h]
        )
        sent[h] = flip(out, "col", 4)
    (share,) = run_segment(("pair", 0), "share", w[4], [kept[0], sent[0]], [low], unroll=4)
    (out,) = run_segment(("pair", 1), "low", w[4], [kept[1], sent[1]], [share, low])
    return out.reshape(amplitudes.shape)


def solution(mesh):
    placed = (P(None, "row", "col", None), P(), P())
    return jax.shard_map(
        circuit, mesh=mesh, in_specs=placed, out_specs=P(None, "row", "col", None), check_vma=False
    )
```

```python
import functools

import jax
import jax.numpy as jnp
from jax import lax
from jax.experimental import pallas as pl
from jax.experimental.pallas import tpu as pltpu
from jax.sharding import PartitionSpec as P


F32 = jnp.float32
BF16 = jnp.bfloat16
GD = 128
HALF = 64
LIMIT = 16 << 20
STATE = (16, 16, 8, 128)
PART = (8, 16, 8, 128)


def split(value):
    high = value.astype(BF16)
    return high, (value - high.astype(F32)).astype(BF16)


def onehot(kind, perm_ref):
    row = lax.axis_index("row")
    col = lax.axis_index("col")
    new = lax.broadcasted_iota(jnp.int32, (GD, GD), 0)
    old = lax.broadcasted_iota(jnp.int32, (GD, GD), 1)
    z_own, x_own, c_own = row >> 3, (row >> 1) & 3, row & 1
    rest, core, block = new & 3, (new >> 2) & 1, new >> 3
    if kind == "mid":
        want = ((new & 7) << 4) | (new >> 3)
    elif kind[:3] == "xor":
        want = new ^ ({"xor2": c_own, "xor3": row >> 4, "xor4": col >> 2}[kind] << 6)
    elif kind == "dest":
        x = ((block >> 2) + x_own) & 3
        z = ((block & 3) + z_own) & 3
        want = (((((z << 2) | x) << 1) | (core ^ c_own)) << 2) | rest
    else:
        z = (z_own - (block >> 2)) & 3
        x = (x_own - (block & 3)) & 3
        want = (((((z << 2) | x) << 1) | (core ^ c_own)) << 2) | rest
        state = lax.broadcasted_iota(jnp.int32, (1, GD), 1)
        moved = state & 3
        for t in range(32):
            moved += jnp.where(state >> 2 == t, perm_ref[t] * 4, 0)
        old = jnp.broadcast_to(moved, (GD, GD))
    return jnp.where(want == old, 1.0, 0.0).astype(BF16)


def weight_kernel(kinds, n_prefetch, *refs):
    perm_ref = refs[0] if n_prefetch else None
    gates_ref, out_ref = refs[n_prefetch], refs[-1]
    made = {}
    for number, (rows, cols) in enumerate(kinds):
        for kind in (rows, cols):
            if kind is not None and kind not in made:
                made[kind] = onehot(kind, perm_ref)
        slot = (0, 1, 3)[number]
        real_high, real_low = split(gates_ref[0, slot, 0])
        imag_high, imag_low = split(gates_ref[0, slot, 1])
        wide = jnp.concatenate([real_high, imag_high, real_low, imag_low], axis=1)
        if rows is not None:
            wide = jnp.dot(made[rows], wide, preferred_element_type=F32).astype(BF16)
        parts = [wide[:, GD * i : GD * (i + 1)] for i in range(4)]
        if cols is not None:
            tall = lax.dot_general(
                jnp.concatenate(parts, axis=0),
                made[cols],
                (((1,), (1,)), ((), ())),
                preferred_element_type=F32,
            ).astype(BF16)
            parts = [tall[GD * i : GD * (i + 1)] for i in range(4)]
        out_ref[number, 0:GD, 0:GD] = parts[0]
        out_ref[number, 0:GD, GD:] = parts[1]
        out_ref[number, GD:, 0:GD] = parts[2]
        out_ref[number, GD:, GD:] = parts[3]


def weights(gate_matrices, seg, kinds, permutation):
    prefetch = () if permutation is None else (permutation,)
    block = seg
    if seg == 0:
        block, gate_matrices = 0, gate_matrices[:1]
    return pl.pallas_call(
        functools.partial(weight_kernel, kinds, len(prefetch)),
        out_shape=jax.ShapeDtypeStruct((3, 256, 256), BF16),
        grid_spec=pltpu.PrefetchScalarGridSpec(
            num_scalar_prefetch=len(prefetch),
            grid=(1,),
            in_specs=[pl.BlockSpec((1, 4, 2, GD, GD), lambda i, *_: (block, 0, 0, 0, 0))],
            out_specs=pl.BlockSpec(memory_space=pltpu.VMEM),
        ),
        cost_estimate=pl.CostEstimate(
            flops=3 * 2 * 640 * 128 * 512, bytes_accessed=1 << 20, transcendentals=0
        ),
        compiler_params=pltpu.CompilerParams(vmem_limit_bytes=LIMIT),
    )(*prefetch, gate_matrices)


def low_kernel(gates_ref, out_ref, total_ref):
    seg = pl.program_id(0)
    real, imag = gates_ref[0, 0, 0], gates_ref[0, 0, 1]
    form = jnp.concatenate(
        [jnp.concatenate([real, -imag], axis=1), jnp.concatenate([imag, real], axis=1)], axis=0
    )

    @pl.when(seg == 0)
    def _():
        new = lax.broadcasted_iota(jnp.int32, (256, 256), 0)
        old = lax.broadcasted_iota(jnp.int32, (256, 256), 1)
        want = (((new >> 6) & 1) << 7) | ((new >> 7) << 6) | (new & 63)
        total_ref[...] = jnp.where(want == old, 1.0, 0.0)

    high, low = split(total_ref[...])
    form_high, form_low = split(form)

    def times(left, right):
        return lax.dot_general(
            left, right, (((1,), (1,)), ((), ())), preferred_element_type=F32
        )

    total = times(high, form_high) + (times(high, form_low) + times(low, form_high))
    total_ref[...] = total
    for k, piece in enumerate(split(total)):
        for h in range(2):
            rows = piece[GD * h : GD * (h + 1)]
            out_ref[h, k, 0:GD] = rows
            out_ref[h, k, GD:] = rows


def low_weights(gate_matrices):
    return pl.pallas_call(
        low_kernel,
        out_shape=jax.ShapeDtypeStruct((2, 2, 256, 256), BF16),
        grid=(gate_matrices.shape[0],),
        in_specs=[pl.BlockSpec((1, 1, 2, GD, GD), lambda i: (i, 2, 0, 0, 0))],
        out_specs=pl.BlockSpec(memory_space=pltpu.VMEM),
        scratch_shapes=[pltpu.VMEM((256, 256), F32)],
        cost_estimate=pl.CostEstimate(
            flops=5 * 3 * 2 * 256**3, bytes_accessed=1 << 20, transcendentals=0
        ),
        compiler_params=pltpu.CompilerParams(vmem_limit_bytes=LIMIT),
        name="low_weights",
    )(gate_matrices)


def gate_step(first, second, w_high_low, w_high, sign):
    state = jnp.concatenate([first, second], axis=1)
    turned = jnp.concatenate(
        [pltpu.roll(first, HALF, 1) * sign, pltpu.roll(second, HALF, 1) * sign], axis=1
    )
    high, low = split(jnp.concatenate([state, turned], axis=0))
    both = jnp.dot(w_high_low, high, preferred_element_type=F32)
    small = jnp.dot(w_high, low, preferred_element_type=F32)
    return both[:GD] + (both[GD:] + small)


def segment_kernel(source, target, n_in, unroll, *refs):
    w_ref = refs[0]
    ins = refs[1 : 1 + n_in]
    outs = refs[1 + n_in : -2]
    one, two = refs[-2:]
    lane = lax.broadcasted_iota(jnp.int32, (1, GD), 1)
    sign = jnp.where(lane < HALF, -1.0, 1.0)
    upper = lax.broadcasted_iota(jnp.int32, (1, 8, GD), 1) >= 4

    def load_start(i):
        blocks = []
        for p in (2 * i, 2 * i + 1):
            re = ins[0][0, pl.ds(p, GD, stride=16), :]
            im = ins[0][1, pl.ds(p, GD, stride=16), :]
            if source[1] == 0:
                blocks.append(jnp.where(lane < HALF, re, pltpu.roll(im, HALF, 1)))
            else:
                blocks.append(jnp.where(lane < HALF, pltpu.roll(re, HALF, 1), im))
        return blocks

    def load_pair(i):
        return [
            jnp.concatenate(
                [ins[0][:, p].reshape(HALF, GD), ins[1][:, p].reshape(HALF, GD)], axis=0
            )
            for p in (2 * i, 2 * i + 1)
        ]

    def load_remap(i):
        def half(c):
            if source[1] == "by_x":
                return jnp.stack([ins[x][c, z, i] for z in range(4) for x in range(4)], axis=0)
            return jnp.concatenate([ins[z][c, :, i] for z in range(4)], axis=0)

        near, far = half(0), half(1)
        even = jnp.where(upper, pltpu.roll(far, 4, 1), near)
        odd = jnp.where(upper, far, pltpu.roll(near, 4, 1))
        return [even.reshape(GD, GD), odd.reshape(GD, GD)]

    load = {"start": load_start, "pair": load_pair, "remap": load_remap}[source[0]]

    def top_first(i, carry):
        first, second = load(i)
        result = gate_step(first, second, w_ref[0], w_ref[0, :GD], sign)
        one[:, 2 * i] = result[:, :GD].reshape(16, 8, GD)
        one[:, 2 * i + 1] = result[:, GD:].reshape(16, 8, GD)
        return carry

    def mid(i, carry):
        first = one[2 * i].reshape(GD, GD)
        second = one[2 * i + 1].reshape(GD, GD)
        result = gate_step(first, second, w_ref[1], w_ref[1, :GD], sign)
        two[2 * i] = result[:, :GD].reshape(16, 8, GD)
        two[2 * i + 1] = result[:, GD:].reshape(16, 8, GD)
        return carry

    def top_last(i, carry):
        first = two[:, 2 * i].reshape(GD, GD)
        second = two[:, 2 * i + 1].reshape(GD, GD)
        result = gate_step(first, second, w_ref[2], w_ref[2, :GD], sign)
        pieces = (result[:, :GD], result[:, GD:])
        if target == "pair":
            for p, piece in zip((2 * i, 2 * i + 1), pieces):
                outs[0][:, p] = piece[:HALF].reshape(8, 8, GD)
                outs[1][:, p] = piece[HALF:].reshape(8, 8, GD)
        elif target == "remap":
            even, odd = (piece.reshape(16, 8, GD) for piece in pieces)
            outs[0][:, i] = jnp.where(upper, pltpu.roll(odd, 4, 1), even)
            outs[1][:, i] = jnp.where(upper, odd, pltpu.roll(even, 4, 1))
        else:
            for p, piece in zip((2 * i, 2 * i + 1), pieces):
                one[:, p] = piece.reshape(16, 8, GD)
        return carry

    def low_gate(i, carry):
        low_ref = ins[-1]
        rows = jnp.concatenate([one[:, 4 * i + k].reshape(GD, GD) for k in range(4)], axis=0)
        pair = jnp.concatenate(split(rows), axis=1)
        done = jnp.dot(pair, low_ref[source[1], 0], preferred_element_type=F32) + jnp.dot(
            pair, low_ref[source[1], 1], preferred_element_type=F32
        )
        if target == "share":
            outs[0][i] = done
            return carry
        done = done + ins[-2][i]
        for k in range(4):
            piece = done[GD * k : GD * (k + 1)]
            outs[0][0, pl.ds(4 * i + k, GD, stride=16), :] = piece[:, :GD]
            outs[0][1, pl.ds(4 * i + k, GD, stride=16), :] = piece[:, GD:]
        return carry

    for step in (top_first, mid, top_last):
        lax.fori_loop(0, 8, step, 0, unroll=unroll)
    if target in ("share", "low"):
        lax.fori_loop(0, 4, low_gate, 0, unroll=4 if unroll == 8 else 1)


def run_segment(source, target, w, ins, extra=(), unroll=8):
    if target == "pair":
        out_shape = [jax.ShapeDtypeStruct(PART, F32)] * 2
    elif target == "remap":
        out_shape = [jax.ShapeDtypeStruct((16, 8, 8, 128), F32)] * 2
    elif target == "share":
        out_shape = [jax.ShapeDtypeStruct((4, 512, 256), F32)]
    else:
        out_shape = [jax.ShapeDtypeStruct((2, 2048, 128), F32)]
    args = list(ins) + list(extra)
    vmem = pl.BlockSpec(memory_space=pltpu.VMEM)
    return pl.pallas_call(
        functools.partial(segment_kernel, source, target, len(args), unroll),
        out_shape=out_shape,
        in_specs=[vmem] * (1 + len(args)),
        out_specs=[vmem] * len(out_shape),
        scratch_shapes=[pltpu.VMEM(STATE, F32)] * 2,
        cost_estimate=pl.CostEstimate(
            flops=3 * 3 * 2 * 128 * 256 * 2048, bytes_accessed=3 << 20, transcendentals=0
        ),
        compiler_params=pltpu.CompilerParams(vmem_limit_bytes=LIMIT),
    )(w, *args)


def regroup_kernel(order, *refs):
    ins, outs = refs[:-4], refs[-4:]
    for j in range(4):
        for k in range(4):
            for c in range(2):
                if order == "swap":
                    outs[j][c, k] = ins[k][c, j]
                else:
                    outs[j][c, k] = ins[c][4 * j + k if order == "by_x" else 4 * k + j]


def regroup(order, blocks):
    vmem = pl.BlockSpec(memory_space=pltpu.VMEM)
    return pl.pallas_call(
        functools.partial(regroup_kernel, order),
        out_shape=[jax.ShapeDtypeStruct((2, 4, 8, 8, 128), F32)] * 4,
        in_specs=[vmem] * len(blocks),
        out_specs=[vmem] * 4,
        cost_estimate=pl.CostEstimate(flops=0, bytes_accessed=2 << 20, transcendentals=0),
        compiler_params=pltpu.CompilerParams(vmem_limit_bytes=LIMIT),
    )(*blocks)


def flip(value, axis, mask):
    return lax.ppermute(value, axis, [(s, s ^ mask) for s in range(lax.axis_size(axis))])


def shift_row(value, z, x, c):
    pairs = []
    for s in range(32):
        to = ((((s >> 3) + z) & 3) << 3) | ((((s >> 1) + x) & 3) << 1) | ((s & 1) ^ c)
        pairs.append((s, to))
    return lax.ppermute(value, "row", pairs)


def shift_x(blocks):
    moved = [blocks[0]]
    for x in range(1, 4):
        moved.append(shift_row(blocks[x], 0, x, 0))
    return moved


def shift_z(blocks):
    moved = [blocks[0]]
    for z in range(1, 4):
        moved.append(shift_row(blocks[z], z, 0, 0))
    return moved


def circuit(amplitudes, gate_matrices, permutation):
    state = amplitudes.reshape(2, 2048, 128)
    mid = ("mid", "mid")
    kinds = (
        ((None, None), mid, ("xor2", None)),
        ((None, "xor2"), mid, ("xor3", None)),
        ((None, "xor3"), mid, ("dest", None)),
        ((None, "src"), mid, ("xor4", None)),
        ((None, "xor4"), mid, (None, None)),
    )
    w = [
        weights(gate_matrices, seg, kinds[seg], permutation if seg == 3 else None)
        for seg in range(5)
    ]
    low = low_weights(gate_matrices)
    halves = (0, 1)
    kept, sent = {}, {}
    for h in halves:
        kept[h], out = run_segment(("start", h), "pair", w[0], [state])
        sent[h] = flip(out, "row", 1)
    for h in halves:
        kept[h], out = run_segment(("pair",), "pair", w[1], [kept[h], sent[h]])
        sent[h] = flip(out, "row", 16)
    got = {}
    for h in halves:
        near, far = run_segment(("pair",), "remap", w[2], [kept[h], sent[h]])
        pair = [near, flip(far, "row", 1)]
        if h == 0:
            moved = shift_z(regroup("by_z", pair))
            got[h] = shift_x(regroup("swap", moved))
        else:
            moved = shift_x(regroup("by_x", pair))
            got[h] = shift_z(regroup("swap", moved))
    for h in halves:
        kept[h], out = run_segment(("remap", ("by_x", "by_z")[h]), "pair", w[3], got[h])
        sent[h] = flip(out, "col", 4)
    (share,) = run_segment(("pair", 0), "share", w[4], [kept[0], sent[0]], [low], unroll=4)
    (out,) = run_segment(("pair", 1), "low", w[4], [kept[1], sent[1]], [share, low])
    return out.reshape(amplitudes.shape)


def solution(mesh):
    placed = (P(None, "row", "col", None), P(), P())
    return jax.shard_map(
        circuit, mesh=mesh, in_specs=placed, out_specs=P(None, "row", "col", None), check_vma=False
    )
```

```python
import functools

import jax
import jax.numpy as jnp
from jax import lax
from jax.experimental import pallas as pl
from jax.experimental.pallas import tpu as pltpu
from jax.sharding import PartitionSpec as P


F32 = jnp.float32
BF16 = jnp.bfloat16
GD = 128
HALF = 64
LIMIT = 16 << 20
STATE = (16, 16, 8, 128)
PART = (8, 16, 8, 128)


def split(value):
    high = value.astype(BF16)
    return high, (value - high.astype(F32)).astype(BF16)


def onehot(kind, perm_ref):
    row = lax.axis_index("row")
    col = lax.axis_index("col")
    new = lax.broadcasted_iota(jnp.int32, (GD, GD), 0)
    old = lax.broadcasted_iota(jnp.int32, (GD, GD), 1)
    z_own, x_own, c_own = row >> 3, (row >> 1) & 3, row & 1
    rest, core, block = new & 3, (new >> 2) & 1, new >> 3
    if kind == "mid":
        want = ((new & 7) << 4) | (new >> 3)
    elif kind[:3] == "xor":
        want = new ^ ({"xor2": c_own, "xor4": col >> 2}[kind] << 6)
    elif kind == "dest":
        x = ((block >> 2) + x_own) & 3
        z = ((block & 3) + z_own) & 3
        want = (((((z << 2) | x) << 1) | (core ^ c_own)) << 2) | rest
    else:
        z = ((block >> 3) << 1) | ((z_own - (block >> 2)) & 1)
        x = (x_own - (block & 3)) & 3
        want = (((((z << 2) | x) << 1) | (core ^ c_own)) << 2) | rest
        state = lax.broadcasted_iota(jnp.int32, (1, GD), 1)
        moved = state & 3
        for t in range(32):
            moved += jnp.where(state >> 2 == t, perm_ref[t] * 4, 0)
        old = jnp.broadcast_to(moved, (GD, GD))
    return jnp.where(want == old, 1.0, 0.0).astype(BF16)


def weight_kernel(kinds, n_prefetch, *refs):
    perm_ref = refs[0] if n_prefetch else None
    gates_ref, out_ref = refs[n_prefetch], refs[-1]
    made = {}
    for number, (rows, cols) in enumerate(kinds):
        for kind in (rows, cols):
            if kind is not None and kind not in made:
                made[kind] = onehot(kind, perm_ref)
        slot = (0, 1, 3)[number]
        real_high, real_low = split(gates_ref[0, slot, 0])
        imag_high, imag_low = split(gates_ref[0, slot, 1])
        wide = jnp.concatenate([real_high, imag_high, real_low, imag_low], axis=1)
        if rows is not None:
            wide = jnp.dot(made[rows], wide, preferred_element_type=F32).astype(BF16)
        parts = [wide[:, GD * i : GD * (i + 1)] for i in range(4)]
        if cols is not None:
            tall = lax.dot_general(
                jnp.concatenate(parts, axis=0),
                made[cols],
                (((1,), (1,)), ((), ())),
                preferred_element_type=F32,
            ).astype(BF16)
            parts = [tall[GD * i : GD * (i + 1)] for i in range(4)]
        out_ref[number, 0:GD, 0:GD] = parts[0]
        out_ref[number, 0:GD, GD:] = parts[1]
        out_ref[number, GD:, 0:GD] = parts[2]
        out_ref[number, GD:, GD:] = parts[3]


def weights(gate_matrices, seg, kinds, permutation):
    prefetch = () if permutation is None else (permutation,)
    block = seg
    if seg == 0:
        block, gate_matrices = 0, gate_matrices[:1]
    return pl.pallas_call(
        functools.partial(weight_kernel, kinds, len(prefetch)),
        out_shape=jax.ShapeDtypeStruct((3, 256, 256), BF16),
        grid_spec=pltpu.PrefetchScalarGridSpec(
            num_scalar_prefetch=len(prefetch),
            grid=(1,),
            in_specs=[pl.BlockSpec((1, 4, 2, GD, GD), lambda i, *_: (block, 0, 0, 0, 0))],
            out_specs=pl.BlockSpec(memory_space=pltpu.VMEM),
        ),
        cost_estimate=pl.CostEstimate(
            flops=3 * 2 * 640 * 128 * 512, bytes_accessed=1 << 20, transcendentals=0
        ),
        compiler_params=pltpu.CompilerParams(vmem_limit_bytes=LIMIT),
    )(*prefetch, gate_matrices)


def low_kernel(gates_ref, out_ref, total_ref):
    seg = pl.program_id(0)
    real, imag = gates_ref[0, 0, 0], gates_ref[0, 0, 1]
    form = jnp.concatenate(
        [jnp.concatenate([real, -imag], axis=1), jnp.concatenate([imag, real], axis=1)], axis=0
    )

    @pl.when(seg == 0)
    def _():
        new = lax.broadcasted_iota(jnp.int32, (256, 256), 0)
        old = lax.broadcasted_iota(jnp.int32, (256, 256), 1)
        want = (((new >> 6) & 1) << 7) | (((new >> 5) & 1) << 6) | ((new >> 7) << 5) | (new & 31)
        total_ref[...] = jnp.where(want == old, 1.0, 0.0)

    high, low = split(total_ref[...])
    form_high, form_low = split(form)

    def times(left, right):
        return lax.dot_general(
            left, right, (((1,), (1,)), ((), ())), preferred_element_type=F32
        )

    total = times(high, form_high) + (times(high, form_low) + times(low, form_high))
    total_ref[...] = total
    for k, piece in enumerate(split(total)):
        for h in range(2):
            rows = piece[GD * h : GD * (h + 1)]
            out_ref[h, k, 0:GD] = rows
            out_ref[h, k, GD:] = rows


def low_weights(gate_matrices):
    return pl.pallas_call(
        low_kernel,
        out_shape=jax.ShapeDtypeStruct((2, 2, 256, 256), BF16),
        grid=(gate_matrices.shape[0],),
        in_specs=[pl.BlockSpec((1, 1, 2, GD, GD), lambda i: (i, 2, 0, 0, 0))],
        out_specs=pl.BlockSpec(memory_space=pltpu.VMEM),
        scratch_shapes=[pltpu.VMEM((256, 256), F32)],
        cost_estimate=pl.CostEstimate(
            flops=5 * 3 * 2 * 256**3, bytes_accessed=1 << 20, transcendentals=0
        ),
        compiler_params=pltpu.CompilerParams(vmem_limit_bytes=LIMIT),
        name="low_weights",
    )(gate_matrices)


def cross(first, second, step):
    axis = first.ndim - 1
    lane = lax.broadcasted_iota(jnp.int32, (1,) * axis + (GD,), axis)
    off = (lane & step) == 0
    return (
        jnp.where(off, first, pltpu.roll(second, step, axis)),
        jnp.where(off, pltpu.roll(first, GD - step, axis), second),
    )


def in_order(swapped, first, second):
    return jnp.where(swapped, second, first), jnp.where(swapped, first, second)


def pack_kernel(state_ref, *outs):
    own = lax.axis_index("row") >> 4 == 1

    def some(p, carry):
        tops = []
        for top in range(2):
            rows = [state_ref[c, pl.ds(1024 * top + p, HALF, stride=16), :] for c in range(2)]
            tops.append(cross(rows[0], rows[1], 64))
        sides = [cross(tops[0][b], tops[1][b], 32) for b in range(2)]
        for h in range(2):
            stays, leaves = in_order(own, sides[0][h], sides[1][h])
            outs[2 * h][:, p] = stays.reshape(8, 8, GD)
            outs[2 * h + 1][:, p] = leaves.reshape(8, 8, GD)
        return carry

    lax.fori_loop(0, 16, some, 0, unroll=8)


def pack(state):
    vmem = pl.BlockSpec(memory_space=pltpu.VMEM)
    return pl.pallas_call(
        pack_kernel,
        out_shape=[jax.ShapeDtypeStruct(PART, F32)] * 4,
        in_specs=[vmem],
        out_specs=[vmem] * 4,
        cost_estimate=pl.CostEstimate(flops=0, bytes_accessed=4 << 20, transcendentals=0),
        compiler_params=pltpu.CompilerParams(vmem_limit_bytes=LIMIT),
        name="pack",
    )(state)


def gate_step(first, second, w_high_low, w_high, sign):
    state = jnp.concatenate([first, second], axis=1)
    turned = jnp.concatenate(
        [pltpu.roll(first, HALF, 1) * sign, pltpu.roll(second, HALF, 1) * sign], axis=1
    )
    high, low = split(jnp.concatenate([state, turned], axis=0))
    both = jnp.dot(w_high_low, high, preferred_element_type=F32)
    small = jnp.dot(w_high, low, preferred_element_type=F32)
    return both[:GD] + (both[GD:] + small)


def segment_kernel(source, target, n_in, unroll, *refs):
    w_ref = refs[0]
    ins = refs[1 : 1 + n_in]
    outs = refs[1 + n_in : -2]
    one, two = refs[-2:]
    lane = lax.broadcasted_iota(jnp.int32, (1, GD), 1)
    sign = jnp.where(lane < HALF, -1.0, 1.0)
    upper = lax.broadcasted_iota(jnp.int32, (1, 8, GD), 1) >= 4

    def load_start(i):
        own = lax.axis_index("row") >> 4 == 1
        blocks = []
        for p in (2 * i, 2 * i + 1):
            sides = in_order(own, ins[0][:, p].reshape(HALF, GD), ins[1][:, p].reshape(HALF, GD))
            blocks.append(jnp.concatenate(cross(*sides, 32), axis=0))
        return blocks

    def load_turn(i):
        blocks = []
        for p in (2 * i, 2 * i + 1):
            sides = ins[0][:8, p].reshape(HALF, GD), ins[0][8:, p].reshape(HALF, GD)
            blocks.append(jnp.concatenate(cross(*sides, 32), axis=0))
        return blocks

    def load_pair(i):
        return [
            jnp.concatenate(
                [ins[0][:, p].reshape(HALF, GD), ins[1][:, p].reshape(HALF, GD)], axis=0
            )
            for p in (2 * i, 2 * i + 1)
        ]

    def load_remap(i):
        def half(c):
            if source[1] == "by_x":
                return jnp.stack([ins[x][c, z, i] for z in range(4) for x in range(4)], axis=0)
            return jnp.concatenate([ins[z][c, :, i] for z in range(4)], axis=0)

        near, far = half(0), half(1)
        even = jnp.where(upper, pltpu.roll(far, 4, 1), near)
        odd = jnp.where(upper, far, pltpu.roll(near, 4, 1))
        z_own = lax.axis_index("row") >> 3
        blocks = []
        for rows in (even, odd):
            near_rows = [], []
            for z in range(2):
                swapped = ((z_own - z) & 3) >= 2
                sides = in_order(swapped, rows[4 * z : 4 * z + 4], rows[4 * z + 8 : 4 * z + 12])
                for k, side in enumerate(cross(*sides, 32)):
                    near_rows[k].append(side)
            blocks.append(jnp.concatenate(near_rows[0] + near_rows[1], axis=0).reshape(GD, GD))
        return blocks

    load = {
        "start": load_start,
        "pair": load_pair,
        "turn": load_turn,
        "remap": load_remap,
    }[source[0]]

    def top_first(i, carry):
        first, second = load(i)
        result = gate_step(first, second, w_ref[0], w_ref[0, :GD], sign)
        one[:, 2 * i] = result[:, :GD].reshape(16, 8, GD)
        one[:, 2 * i + 1] = result[:, GD:].reshape(16, 8, GD)
        return carry

    def mid(i, carry):
        first = one[2 * i].reshape(GD, GD)
        second = one[2 * i + 1].reshape(GD, GD)
        result = gate_step(first, second, w_ref[1], w_ref[1, :GD], sign)
        two[2 * i] = result[:, :GD].reshape(16, 8, GD)
        two[2 * i + 1] = result[:, GD:].reshape(16, 8, GD)
        return carry

    def top_last(i, carry):
        first = two[:, 2 * i].reshape(GD, GD)
        second = two[:, 2 * i + 1].reshape(GD, GD)
        result = gate_step(first, second, w_ref[2], w_ref[2, :GD], sign)
        pieces = (result[:, :GD], result[:, GD:])
        if target == "pair":
            for p, piece in zip((2 * i, 2 * i + 1), pieces):
                outs[0][:, p] = piece[:HALF].reshape(8, 8, GD)
                outs[1][:, p] = piece[HALF:].reshape(8, 8, GD)
        elif target == "remap":
            even, odd = (piece.reshape(16, 8, GD) for piece in pieces)
            outs[0][:, i] = jnp.where(upper, pltpu.roll(odd, 4, 1), even)
            outs[1][:, i] = jnp.where(upper, odd, pltpu.roll(even, 4, 1))
        else:
            held = outs[0] if target == "plain" else one
            for p, piece in zip((2 * i, 2 * i + 1), pieces):
                held[:, p] = piece.reshape(16, 8, GD)
        return carry

    def low_gate(i, carry):
        low_ref = ins[-1]
        rows = jnp.concatenate([one[:, 4 * i + k].reshape(GD, GD) for k in range(4)], axis=0)
        pair = jnp.concatenate(split(rows), axis=1)
        done = jnp.dot(pair, low_ref[source[1], 0], preferred_element_type=F32) + jnp.dot(
            pair, low_ref[source[1], 1], preferred_element_type=F32
        )
        if target == "share":
            outs[0][i] = done
            return carry
        done = done + ins[-2][i]
        for k in range(4):
            piece = done[GD * k : GD * (k + 1)]
            outs[0][0, pl.ds(4 * i + k, GD, stride=16), :] = piece[:, :GD]
            outs[0][1, pl.ds(4 * i + k, GD, stride=16), :] = piece[:, GD:]
        return carry

    for step in (top_first, mid, top_last):
        lax.fori_loop(0, 8, step, 0, unroll=unroll)
    if target in ("share", "low"):
        lax.fori_loop(0, 4, low_gate, 0, unroll=4 if unroll == 8 else 1)


def run_segment(source, target, w, ins, extra=(), unroll=8):
    if target == "pair":
        out_shape = [jax.ShapeDtypeStruct(PART, F32)] * 2
    elif target == "remap":
        out_shape = [jax.ShapeDtypeStruct((16, 8, 8, 128), F32)] * 2
    elif target == "plain":
        out_shape = [jax.ShapeDtypeStruct(STATE, F32)]
    elif target == "share":
        out_shape = [jax.ShapeDtypeStruct((4, 512, 256), F32)]
    else:
        out_shape = [jax.ShapeDtypeStruct((2, 2048, 128), F32)]
    args = list(ins) + list(extra)
    vmem = pl.BlockSpec(memory_space=pltpu.VMEM)
    return pl.pallas_call(
        functools.partial(segment_kernel, source, target, len(args), unroll),
        out_shape=out_shape,
        in_specs=[vmem] * (1 + len(args)),
        out_specs=[vmem] * len(out_shape),
        scratch_shapes=[pltpu.VMEM(STATE, F32)] * 2,
        cost_estimate=pl.CostEstimate(
            flops=3 * 3 * 2 * 128 * 256 * 2048, bytes_accessed=3 << 20, transcendentals=0
        ),
        compiler_params=pltpu.CompilerParams(vmem_limit_bytes=LIMIT),
    )(w, *args)


def regroup_kernel(order, *refs):
    ins, outs = refs[:-4], refs[-4:]
    for j in range(4):
        for k in range(4):
            for c in range(2):
                if order == "swap":
                    outs[j][c, k] = ins[k][c, j]
                else:
                    outs[j][c, k] = ins[c][4 * j + k if order == "by_x" else 4 * k + j]


def regroup(order, blocks):
    vmem = pl.BlockSpec(memory_space=pltpu.VMEM)
    return pl.pallas_call(
        functools.partial(regroup_kernel, order),
        out_shape=[jax.ShapeDtypeStruct((2, 4, 8, 8, 128), F32)] * 4,
        in_specs=[vmem] * len(blocks),
        out_specs=[vmem] * 4,
        cost_estimate=pl.CostEstimate(flops=0, bytes_accessed=2 << 20, transcendentals=0),
        compiler_params=pltpu.CompilerParams(vmem_limit_bytes=LIMIT),
    )(*blocks)


def flip(value, axis, mask):
    return lax.ppermute(value, axis, [(s, s ^ mask) for s in range(lax.axis_size(axis))])


def shift_row(value, z, x, c):
    pairs = []
    for s in range(32):
        to = ((((s >> 3) + z) & 3) << 3) | ((((s >> 1) + x) & 3) << 1) | ((s & 1) ^ c)
        pairs.append((s, to))
    return lax.ppermute(value, "row", pairs)


def shift_x(blocks):
    moved = [blocks[0]]
    for x in range(1, 4):
        moved.append(shift_row(blocks[x], 0, x, 0))
    return moved


def shift_z(blocks):
    moved = [blocks[0]]
    for z in range(1, 4):
        moved.append(shift_row(blocks[z], z, 0, 0))
    return moved


def circuit(amplitudes, gate_matrices, permutation):
    state = amplitudes.reshape(2, 2048, 128)
    mid = ("mid", "mid")
    kinds = (
        ((None, None), mid, ("xor2", None)),
        ((None, "xor2"), mid, (None, None)),
        ((None, None), mid, ("dest", None)),
        ((None, "src"), mid, ("xor4", None)),
        ((None, "xor4"), mid, (None, None)),
    )
    w = [
        weights(gate_matrices, seg, kinds[seg], permutation if seg == 3 else None)
        for seg in range(5)
    ]
    low = low_weights(gate_matrices)
    halves = (0, 1)
    kept, sent, got = {}, {}, {}
    stays_0, leaves_0, stays_1, leaves_1 = pack(state)
    pairs = ([stays_0, flip(leaves_0, "row", 16)], [stays_1, flip(leaves_1, "row", 16)])
    for h in halves:
        kept[h], out = run_segment(("start",), "pair", w[0], pairs[h])
        sent[h] = flip(out, "row", 1)
        (whole,) = run_segment(("pair",), "plain", w[1], [kept[h], sent[h]])
        near, far = run_segment(("turn",), "remap", w[2], [whole])
        pair = [near, flip(far, "row", 1)]
        if h == 0:
            moved = shift_z(regroup("by_z", pair))
            got[h] = shift_x(regroup("swap", moved))
        else:
            moved = shift_x(regroup("by_x", pair))
            got[h] = shift_z(regroup("swap", moved))
    for h in halves:
        kept[h], out = run_segment(("remap", ("by_x", "by_z")[h]), "pair", w[3], got[h])
        sent[h] = flip(out, "col", 4)
    (share,) = run_segment(("pair", 0), "share", w[4], [kept[0], sent[0]], [low], unroll=4)
    (out,) = run_segment(("pair", 1), "low", w[4], [kept[1], sent[1]], [share, low])
    return out.reshape(amplitudes.shape)


def solution(mesh):
    placed = (P(None, "row", "col", None), P(), P())
    return jax.shard_map(
        circuit, mesh=mesh, in_specs=placed, out_specs=P(None, "row", "col", None), check_vma=False
    )
```

```python
import functools

import jax
import jax.numpy as jnp
from jax import lax
from jax.experimental import pallas as pl
from jax.experimental.pallas import tpu as pltpu
from jax.sharding import PartitionSpec as P


F32 = jnp.float32
BF16 = jnp.bfloat16
GD = 128
HALF = 64
LIMIT = 16 << 20
STATE = (16, 16, 8, 128)
PART = (8, 16, 8, 128)


def split(value):
    high = value.astype(BF16)
    return high, (value - high.astype(F32)).astype(BF16)


def onehot(kind, perm_ref):
    row = lax.axis_index("row")
    col = lax.axis_index("col")
    new = lax.broadcasted_iota(jnp.int32, (GD, GD), 0)
    old = lax.broadcasted_iota(jnp.int32, (GD, GD), 1)
    z_own, x_own, c_own = row >> 3, (row >> 1) & 3, row & 1
    rest, core, block = new & 3, (new >> 2) & 1, new >> 3
    if kind == "mid":
        want = ((new & 7) << 4) | (new >> 3)
    elif kind[:3] == "xor":
        want = new ^ ({"xor2": c_own, "xor4": col >> 2}[kind] << 6)
    elif kind == "dest":
        x = ((block >> 2) + x_own) & 3
        z = ((block & 3) + z_own) & 3
        want = (((((z << 2) | x) << 1) | (core ^ c_own)) << 2) | rest
    else:
        z = ((block >> 3) << 1) | ((z_own - (block >> 2)) & 1)
        x = (x_own - (block & 3)) & 3
        want = (((((z << 2) | x) << 1) | (core ^ c_own)) << 2) | rest
        state = lax.broadcasted_iota(jnp.int32, (1, GD), 1)
        moved = state & 3
        for t in range(32):
            moved += jnp.where(state >> 2 == t, perm_ref[t] * 4, 0)
        old = jnp.broadcast_to(moved, (GD, GD))
    return jnp.where(want == old, 1.0, 0.0).astype(BF16)


def weight_kernel(kinds, n_prefetch, *refs):
    perm_ref = refs[0] if n_prefetch else None
    gates_ref, out_ref = refs[n_prefetch], refs[-1]
    made = {}
    for number, (rows, cols) in enumerate(kinds):
        for kind in (rows, cols):
            if kind is not None and kind not in made:
                made[kind] = onehot(kind, perm_ref)
        slot = (0, 1, 3)[number]
        real_high, real_low = split(gates_ref[0, slot, 0])
        imag_high, imag_low = split(gates_ref[0, slot, 1])
        wide = jnp.concatenate([real_high, imag_high, real_low, imag_low], axis=1)
        if rows is not None:
            wide = jnp.dot(made[rows], wide, preferred_element_type=F32).astype(BF16)
        parts = [wide[:, GD * i : GD * (i + 1)] for i in range(4)]
        if cols is not None:
            tall = lax.dot_general(
                jnp.concatenate(parts, axis=0),
                made[cols],
                (((1,), (1,)), ((), ())),
                preferred_element_type=F32,
            ).astype(BF16)
            parts = [tall[GD * i : GD * (i + 1)] for i in range(4)]
        out_ref[number, 0:GD, 0:GD] = parts[0]
        out_ref[number, 0:GD, GD:] = parts[1]
        out_ref[number, GD:, 0:GD] = parts[2]
        out_ref[number, GD:, GD:] = parts[3]


def weights(gate_matrices, seg, kinds, permutation):
    prefetch = () if permutation is None else (permutation,)
    block = seg
    if seg == 0:
        block, gate_matrices = 0, gate_matrices[:1]
    return pl.pallas_call(
        functools.partial(weight_kernel, kinds, len(prefetch)),
        out_shape=jax.ShapeDtypeStruct((3, 256, 256), BF16),
        grid_spec=pltpu.PrefetchScalarGridSpec(
            num_scalar_prefetch=len(prefetch),
            grid=(1,),
            in_specs=[pl.BlockSpec((1, 4, 2, GD, GD), lambda i, *_: (block, 0, 0, 0, 0))],
            out_specs=pl.BlockSpec(memory_space=pltpu.VMEM),
        ),
        cost_estimate=pl.CostEstimate(
            flops=3 * 2 * 640 * 128 * 512, bytes_accessed=1 << 20, transcendentals=0
        ),
        compiler_params=pltpu.CompilerParams(vmem_limit_bytes=LIMIT),
    )(*prefetch, gate_matrices)


def low_kernel(gates_ref, out_ref, total_ref):
    seg = pl.program_id(0)
    real, imag = gates_ref[0, 0, 0], gates_ref[0, 0, 1]
    form = jnp.concatenate(
        [jnp.concatenate([real, -imag], axis=1), jnp.concatenate([imag, real], axis=1)], axis=0
    )

    @pl.when(seg == 0)
    def _():
        new = lax.broadcasted_iota(jnp.int32, (256, 256), 0)
        old = lax.broadcasted_iota(jnp.int32, (256, 256), 1)
        want = (((new >> 6) & 1) << 7) | (((new >> 5) & 1) << 6) | ((new >> 7) << 5) | (new & 31)
        total_ref[...] = jnp.where(want == old, 1.0, 0.0)

    high, low = split(total_ref[...])
    form_high, form_low = split(form)

    def times(left, right):
        return lax.dot_general(
            left, right, (((1,), (1,)), ((), ())), preferred_element_type=F32
        )

    total = times(high, form_high) + (times(high, form_low) + times(low, form_high))
    total_ref[...] = total
    for k, piece in enumerate(split(total)):
        for h in range(2):
            rows = piece[GD * h : GD * (h + 1)]
            out_ref[h, k, 0:GD] = rows
            out_ref[h, k, GD:] = rows


def low_weights(gate_matrices):
    return pl.pallas_call(
        low_kernel,
        out_shape=jax.ShapeDtypeStruct((2, 2, 256, 256), BF16),
        grid=(gate_matrices.shape[0],),
        in_specs=[pl.BlockSpec((1, 1, 2, GD, GD), lambda i: (i, 2, 0, 0, 0))],
        out_specs=pl.BlockSpec(memory_space=pltpu.VMEM),
        scratch_shapes=[pltpu.VMEM((256, 256), F32)],
        cost_estimate=pl.CostEstimate(
            flops=5 * 3 * 2 * 256**3, bytes_accessed=1 << 20, transcendentals=0
        ),
        compiler_params=pltpu.CompilerParams(vmem_limit_bytes=LIMIT),
        name="low_weights",
    )(gate_matrices)


def cross(first, second, step):
    axis = first.ndim - 1
    lane = lax.broadcasted_iota(jnp.int32, (1,) * axis + (GD,), axis)
    off = (lane & step) == 0
    return (
        jnp.where(off, first, pltpu.roll(second, step, axis)),
        jnp.where(off, pltpu.roll(first, GD - step, axis), second),
    )


def in_order(swapped, first, second):
    return jnp.where(swapped, second, first), jnp.where(swapped, first, second)


def pack_kernel(state_ref, *outs):
    own = lax.axis_index("row") >> 4 == 1

    def some(p, carry):
        tops = []
        for top in range(2):
            rows = [state_ref[c, pl.ds(1024 * top + p, HALF, stride=16), :] for c in range(2)]
            tops.append(cross(rows[0], rows[1], 64))
        sides = [cross(tops[0][b], tops[1][b], 32)[0] for b in range(2)]
        for out, side in zip(outs[:2], in_order(own, *sides)):
            out[:, p] = side.reshape(8, 8, GD)
        for top in range(2):
            outs[2][8 * top : 8 * top + 8, p] = cross(*tops[top], 32)[1].reshape(8, 8, GD)
        return carry

    lax.fori_loop(0, 16, some, 0, unroll=8)


def pack(state):
    vmem = pl.BlockSpec(memory_space=pltpu.VMEM)
    return pl.pallas_call(
        pack_kernel,
        out_shape=[jax.ShapeDtypeStruct(shape, F32) for shape in (PART, PART, STATE)],
        in_specs=[vmem],
        out_specs=[vmem] * 3,
        cost_estimate=pl.CostEstimate(flops=0, bytes_accessed=4 << 20, transcendentals=0),
        compiler_params=pltpu.CompilerParams(vmem_limit_bytes=LIMIT),
        name="pack",
    )(state)


def gate_step(first, second, w_high_low, w_high, sign):
    state = jnp.concatenate([first, second], axis=1)
    turned = jnp.concatenate(
        [pltpu.roll(first, HALF, 1) * sign, pltpu.roll(second, HALF, 1) * sign], axis=1
    )
    high, low = split(jnp.concatenate([state, turned], axis=0))
    both = jnp.dot(w_high_low, high, preferred_element_type=F32)
    small = jnp.dot(w_high, low, preferred_element_type=F32)
    return both[:GD] + (both[GD:] + small)


def segment_kernel(source, target, n_in, unroll, *refs):
    w_ref = refs[0]
    ins = refs[1 : 1 + n_in]
    outs = refs[1 + n_in : -2]
    one, two = refs[-2:]
    lane = lax.broadcasted_iota(jnp.int32, (1, GD), 1)
    sign = jnp.where(lane < HALF, -1.0, 1.0)
    upper = lax.broadcasted_iota(jnp.int32, (1, 8, GD), 1) >= 4

    own = lax.axis_index("row") >> 4 == 1

    def load_start(i):
        blocks = []
        for p in (2 * i, 2 * i + 1):
            sides = in_order(own, ins[0][:, p].reshape(HALF, GD), ins[1][:, p].reshape(HALF, GD))
            blocks.append(jnp.concatenate(cross(*sides, 32), axis=0))
        return blocks

    def load_whole(i):
        return [ins[0][:, p].reshape(GD, GD) for p in (2 * i, 2 * i + 1)]

    def load_join(i):
        blocks = []
        for p in (2 * i, 2 * i + 1):
            sides = in_order(own, ins[0][:, p].reshape(HALF, GD), ins[1][:, p].reshape(HALF, GD))
            blocks.append(jnp.concatenate(sides, axis=0))
        return blocks

    def load_turn(i):
        blocks = []
        for p in (2 * i, 2 * i + 1):
            sides = ins[0][:8, p].reshape(HALF, GD), ins[0][8:, p].reshape(HALF, GD)
            blocks.append(jnp.concatenate(cross(*sides, 32), axis=0))
        return blocks

    def load_pair(i):
        return [
            jnp.concatenate(
                [ins[0][:, p].reshape(HALF, GD), ins[1][:, p].reshape(HALF, GD)], axis=0
            )
            for p in (2 * i, 2 * i + 1)
        ]

    def load_remap(i):
        def half(c):
            if source[1] == "by_x":
                return jnp.stack([ins[x][c, z, i] for z in range(4) for x in range(4)], axis=0)
            return jnp.concatenate([ins[z][c, :, i] for z in range(4)], axis=0)

        near, far = half(0), half(1)
        even = jnp.where(upper, pltpu.roll(far, 4, 1), near)
        odd = jnp.where(upper, far, pltpu.roll(near, 4, 1))
        z_own = lax.axis_index("row") >> 3
        blocks = []
        for rows in (even, odd):
            near_rows = [], []
            for z in range(2):
                swapped = ((z_own - z) & 3) >= 2
                sides = in_order(swapped, rows[4 * z : 4 * z + 4], rows[4 * z + 8 : 4 * z + 12])
                for k, side in enumerate(cross(*sides, 32)):
                    near_rows[k].append(side)
            blocks.append(jnp.concatenate(near_rows[0] + near_rows[1], axis=0).reshape(GD, GD))
        return blocks

    load = {
        "start": load_start,
        "pair": load_pair,
        "turn": load_turn,
        "whole": load_whole,
        "join": load_join,
        "remap": load_remap,
    }[source[0]]

    def top_first(i, carry):
        first, second = load(i)
        result = gate_step(first, second, w_ref[0], w_ref[0, :GD], sign)
        one[:, 2 * i] = result[:, :GD].reshape(16, 8, GD)
        one[:, 2 * i + 1] = result[:, GD:].reshape(16, 8, GD)
        return carry

    def mid(i, carry):
        first = one[2 * i].reshape(GD, GD)
        second = one[2 * i + 1].reshape(GD, GD)
        result = gate_step(first, second, w_ref[1], w_ref[1, :GD], sign)
        two[2 * i] = result[:, :GD].reshape(16, 8, GD)
        two[2 * i + 1] = result[:, GD:].reshape(16, 8, GD)
        return carry

    def top_last(i, carry):
        first = two[:, 2 * i].reshape(GD, GD)
        second = two[:, 2 * i + 1].reshape(GD, GD)
        result = gate_step(first, second, w_ref[2], w_ref[2, :GD], sign)
        pieces = (result[:, :GD], result[:, GD:])
        if target == "pair":
            for p, piece in zip((2 * i, 2 * i + 1), pieces):
                outs[0][:, p] = piece[:HALF].reshape(8, 8, GD)
                outs[1][:, p] = piece[HALF:].reshape(8, 8, GD)
        elif target == "leave":
            for p, piece in zip((2 * i, 2 * i + 1), pieces):
                sides = in_order(own, *cross(piece[:HALF], piece[HALF:], 32))
                for out, side in zip(outs, sides):
                    out[:, p] = side.reshape(8, 8, GD)
        elif target == "remap":
            even, odd = (piece.reshape(16, 8, GD) for piece in pieces)
            outs[0][:, i] = jnp.where(upper, pltpu.roll(odd, 4, 1), even)
            outs[1][:, i] = jnp.where(upper, odd, pltpu.roll(even, 4, 1))
        else:
            held = outs[0] if target == "plain" else one
            for p, piece in zip((2 * i, 2 * i + 1), pieces):
                held[:, p] = piece.reshape(16, 8, GD)
        return carry

    def low_gate(i, carry):
        low_ref = ins[-1]
        rows = jnp.concatenate([one[:, 4 * i + k].reshape(GD, GD) for k in range(4)], axis=0)
        pair = jnp.concatenate(split(rows), axis=1)
        done = jnp.dot(pair, low_ref[source[1], 0], preferred_element_type=F32) + jnp.dot(
            pair, low_ref[source[1], 1], preferred_element_type=F32
        )
        if target == "share":
            outs[0][i] = done
            return carry
        done = done + ins[-2][i]
        for k in range(4):
            piece = done[GD * k : GD * (k + 1)]
            outs[0][0, pl.ds(4 * i + k, GD, stride=16), :] = piece[:, :GD]
            outs[0][1, pl.ds(4 * i + k, GD, stride=16), :] = piece[:, GD:]
        return carry

    for step in (top_first, mid, top_last):
        lax.fori_loop(0, 8, step, 0, unroll=unroll)
    if target in ("share", "low"):
        lax.fori_loop(0, 4, low_gate, 0, unroll=4 if unroll == 8 else 1)


def run_segment(source, target, w, ins, extra=(), unroll=8):
    if target in ("pair", "leave"):
        out_shape = [jax.ShapeDtypeStruct(PART, F32)] * 2
    elif target == "remap":
        out_shape = [jax.ShapeDtypeStruct((16, 8, 8, 128), F32)] * 2
    elif target == "plain":
        out_shape = [jax.ShapeDtypeStruct(STATE, F32)]
    elif target == "share":
        out_shape = [jax.ShapeDtypeStruct((4, 512, 256), F32)]
    else:
        out_shape = [jax.ShapeDtypeStruct((2, 2048, 128), F32)]
    args = list(ins) + list(extra)
    vmem = pl.BlockSpec(memory_space=pltpu.VMEM)
    return pl.pallas_call(
        functools.partial(segment_kernel, source, target, len(args), unroll),
        out_shape=out_shape,
        in_specs=[vmem] * (1 + len(args)),
        out_specs=[vmem] * len(out_shape),
        scratch_shapes=[pltpu.VMEM(STATE, F32)] * 2,
        cost_estimate=pl.CostEstimate(
            flops=3 * 3 * 2 * 128 * 256 * 2048, bytes_accessed=3 << 20, transcendentals=0
        ),
        compiler_params=pltpu.CompilerParams(vmem_limit_bytes=LIMIT),
    )(w, *args)


def regroup_kernel(order, *refs):
    ins, outs = refs[:-4], refs[-4:]
    for j in range(4):
        for k in range(4):
            for c in range(2):
                if order == "swap":
                    outs[j][c, k] = ins[k][c, j]
                else:
                    outs[j][c, k] = ins[c][4 * j + k if order == "by_x" else 4 * k + j]


def regroup(order, blocks):
    vmem = pl.BlockSpec(memory_space=pltpu.VMEM)
    return pl.pallas_call(
        functools.partial(regroup_kernel, order),
        out_shape=[jax.ShapeDtypeStruct((2, 4, 8, 8, 128), F32)] * 4,
        in_specs=[vmem] * len(blocks),
        out_specs=[vmem] * 4,
        cost_estimate=pl.CostEstimate(flops=0, bytes_accessed=2 << 20, transcendentals=0),
        compiler_params=pltpu.CompilerParams(vmem_limit_bytes=LIMIT),
    )(*blocks)


def flip(value, axis, mask):
    return lax.ppermute(value, axis, [(s, s ^ mask) for s in range(lax.axis_size(axis))])


def shift_row(value, z, x, c):
    pairs = []
    for s in range(32):
        to = ((((s >> 3) + z) & 3) << 3) | ((((s >> 1) + x) & 3) << 1) | ((s & 1) ^ c)
        pairs.append((s, to))
    return lax.ppermute(value, "row", pairs)


def shift_x(blocks):
    moved = [blocks[0]]
    for x in range(1, 4):
        moved.append(shift_row(blocks[x], 0, x, 0))
    return moved


def shift_z(blocks):
    moved = [blocks[0]]
    for z in range(1, 4):
        moved.append(shift_row(blocks[z], z, 0, 0))
    return moved


def circuit(amplitudes, gate_matrices, permutation):
    state = amplitudes.reshape(2, 2048, 128)
    mid = ("mid", "mid")
    kinds = (
        ((None, None), mid, ("xor2", None)),
        ((None, "xor2"), mid, (None, None)),
        ((None, None), mid, ("dest", None)),
        ((None, "src"), mid, ("xor4", None)),
        ((None, "xor4"), mid, (None, None)),
    )
    w = [
        weights(gate_matrices, seg, kinds[seg], permutation if seg == 3 else None)
        for seg in range(5)
    ]
    low = low_weights(gate_matrices)
    halves = (0, 1)
    kept, sent, got = {}, {}, {}
    stays, leaves, whole = pack(state)
    firsts = ("start",), [stays, flip(leaves, "row", 16)]
    for h in halves:
        source, ins = firsts if h == 0 else (("whole",), [whole])
        kept[h], out = run_segment(source, "pair", w[0], ins)
        sent[h] = flip(out, "row", 1)
        pair = [kept[h], sent[h]]
        if h == 0:
            pair = run_segment(("pair",), "plain", w[1], pair)
        else:
            stays, leaves = run_segment(("pair",), "leave", w[1], pair)
            pair = [stays, flip(leaves, "row", 16)]
        near, far = run_segment(("turn", "join")[h : h + 1], "remap", w[2], pair)
        pair = [near, flip(far, "row", 1)]
        if h == 0:
            moved = shift_z(regroup("by_z", pair))
            got[h] = shift_x(regroup("swap", moved))
        else:
            moved = shift_x(regroup("by_x", pair))
            got[h] = shift_z(regroup("swap", moved))
    for h in halves:
        kept[h], out = run_segment(("remap", ("by_x", "by_z")[h]), "pair", w[3], got[h])
        sent[h] = flip(out, "col", 4)
    (share,) = run_segment(("pair", 0), "share", w[4], [kept[0], sent[0]], [low], unroll=4)
    (out,) = run_segment(("pair", 1), "low", w[4], [kept[1], sent[1]], [share, low])
    return out.reshape(amplitudes.shape)


def solution(mesh):
    placed = (P(None, "row", "col", None), P(), P())
    return jax.shard_map(
        circuit, mesh=mesh, in_specs=placed, out_specs=P(None, "row", "col", None), check_vma=False
    )
```

```python
import functools

import jax
import jax.numpy as jnp
from jax import lax
from jax.experimental import pallas as pl
from jax.experimental.pallas import tpu as pltpu
from jax.sharding import PartitionSpec as P


F32 = jnp.float32
BF16 = jnp.bfloat16
GD = 128
HALF = 64
LIMIT = 16 << 20
STATE = (16, 16, 8, 128)
PART = (8, 16, 8, 128)


def split(value):
    high = value.astype(BF16)
    return high, (value - high.astype(F32)).astype(BF16)


def onehot(kind, perm_ref):
    row = lax.axis_index("row")
    col = lax.axis_index("col")
    new = lax.broadcasted_iota(jnp.int32, (GD, GD), 0)
    old = lax.broadcasted_iota(jnp.int32, (GD, GD), 1)
    z_own, x_own, c_own = row >> 3, (row >> 1) & 3, row & 1
    rest, core, block = new & 3, (new >> 2) & 1, new >> 3
    if kind == "mid":
        want = ((new & 7) << 4) | (new >> 3)
    elif kind[:3] == "xor":
        want = new ^ ({"xor2": c_own, "xor4": col >> 2}[kind] << 6)
    elif kind == "dest":
        x = ((block >> 2) + x_own) & 3
        z = ((block & 3) + z_own) & 3
        want = (((((z << 2) | x) << 1) | (core ^ c_own)) << 2) | rest
    else:
        z = ((block >> 3) << 1) | ((z_own - (block >> 2)) & 1)
        x = (x_own - (block & 3)) & 3
        want = (((((z << 2) | x) << 1) | (core ^ c_own)) << 2) | rest
        state = lax.broadcasted_iota(jnp.int32, (1, GD), 1)
        moved = state & 3
        for t in range(32):
            moved += jnp.where(state >> 2 == t, perm_ref[t] * 4, 0)
        old = jnp.broadcast_to(moved, (GD, GD))
    return jnp.where(want == old, 1.0, 0.0).astype(BF16)


def weight_kernel(kinds, n_prefetch, *refs):
    perm_ref = refs[0] if n_prefetch else None
    gates_ref, out_ref = refs[n_prefetch], refs[-1]
    made = {}
    for number, (rows, cols) in enumerate(kinds):
        for kind in (rows, cols):
            if kind is not None and kind not in made:
                made[kind] = onehot(kind, perm_ref)
        slot = (0, 1, 3)[number]
        real_high, real_low = split(gates_ref[0, slot, 0])
        imag_high, imag_low = split(gates_ref[0, slot, 1])
        wide = jnp.concatenate([real_high, imag_high, real_low, imag_low], axis=1)
        if rows is not None:
            wide = jnp.dot(made[rows], wide, preferred_element_type=F32).astype(BF16)
        parts = [wide[:, GD * i : GD * (i + 1)] for i in range(4)]
        if cols is not None:
            tall = lax.dot_general(
                jnp.concatenate(parts, axis=0),
                made[cols],
                (((1,), (1,)), ((), ())),
                preferred_element_type=F32,
            ).astype(BF16)
            parts = [tall[GD * i : GD * (i + 1)] for i in range(4)]
        out_ref[number, 0:GD, 0:GD] = parts[0]
        out_ref[number, 0:GD, GD:] = parts[1]
        out_ref[number, GD:, 0:GD] = parts[2]
        out_ref[number, GD:, GD:] = parts[3]


def weights(gate_matrices, seg, kinds, permutation):
    prefetch = () if permutation is None else (permutation,)
    block = seg
    if seg == 0:
        block, gate_matrices = 0, gate_matrices[:1]
    return pl.pallas_call(
        functools.partial(weight_kernel, kinds, len(prefetch)),
        out_shape=jax.ShapeDtypeStruct((3, 256, 256), BF16),
        grid_spec=pltpu.PrefetchScalarGridSpec(
            num_scalar_prefetch=len(prefetch),
            grid=(1,),
            in_specs=[pl.BlockSpec((1, 4, 2, GD, GD), lambda i, *_: (block, 0, 0, 0, 0))],
            out_specs=pl.BlockSpec(memory_space=pltpu.VMEM),
        ),
        cost_estimate=pl.CostEstimate(
            flops=3 * 2 * 640 * 128 * 512, bytes_accessed=1 << 20, transcendentals=0
        ),
        compiler_params=pltpu.CompilerParams(vmem_limit_bytes=LIMIT),
    )(*prefetch, gate_matrices)


def low_kernel(gates_ref, out_ref, total_ref):
    seg = pl.program_id(0)
    real, imag = gates_ref[0, 0, 0], gates_ref[0, 0, 1]
    form = jnp.concatenate(
        [jnp.concatenate([real, -imag], axis=1), jnp.concatenate([imag, real], axis=1)], axis=0
    )

    @pl.when(seg == 0)
    def _():
        new = lax.broadcasted_iota(jnp.int32, (256, 256), 0)
        old = lax.broadcasted_iota(jnp.int32, (256, 256), 1)
        want = (((new >> 6) & 1) << 7) | (((new >> 5) & 1) << 6) | ((new >> 7) << 5) | (new & 31)
        total_ref[...] = jnp.where(want == old, 1.0, 0.0)

    high, low = split(total_ref[...])
    form_high, form_low = split(form)

    def times(left, right):
        return lax.dot_general(
            left, right, (((1,), (1,)), ((), ())), preferred_element_type=F32
        )

    total = times(high, form_high) + (times(high, form_low) + times(low, form_high))
    total_ref[...] = total
    for k, piece in enumerate(split(total)):
        for h in range(2):
            rows = piece[GD * h : GD * (h + 1)]
            out_ref[h, k, 0:GD] = rows
            out_ref[h, k, GD:] = rows


def low_weights(gate_matrices):
    return pl.pallas_call(
        low_kernel,
        out_shape=jax.ShapeDtypeStruct((2, 2, 256, 256), BF16),
        grid=(gate_matrices.shape[0],),
        in_specs=[pl.BlockSpec((1, 1, 2, GD, GD), lambda i: (i, 2, 0, 0, 0))],
        out_specs=pl.BlockSpec(memory_space=pltpu.VMEM),
        scratch_shapes=[pltpu.VMEM((256, 256), F32)],
        cost_estimate=pl.CostEstimate(
            flops=5 * 3 * 2 * 256**3, bytes_accessed=1 << 20, transcendentals=0
        ),
        compiler_params=pltpu.CompilerParams(vmem_limit_bytes=LIMIT),
        name="low_weights",
    )(gate_matrices)


def cross(first, second, step):
    axis = first.ndim - 1
    lane = lax.broadcasted_iota(jnp.int32, (1,) * axis + (GD,), axis)
    off = (lane & step) == 0
    return (
        jnp.where(off, first, pltpu.roll(second, step, axis)),
        jnp.where(off, pltpu.roll(first, GD - step, axis), second),
    )


def in_order(swapped, first, second):
    return jnp.where(swapped, second, first), jnp.where(swapped, first, second)


def turned(blocks):
    sub = lax.broadcasted_iota(jnp.int32, (1, 8, 1), 1)
    for step in (1, 2, 4):
        off = (sub & step) == 0
        made = [None] * 8
        for k in range(8):
            if k & step:
                continue
            first, second = blocks[k], blocks[k + step]
            made[k] = jnp.where(off, first, pltpu.roll(second, step, 1))
            made[k + step] = jnp.where(off, pltpu.roll(first, 8 - step, 1), second)
        blocks = made
    return blocks


def pack_kernel(state_ref, *outs):
    own = lax.axis_index("row") >> 4 == 1

    def some(a, carry):
        made = [[], [], [], []]
        for o in range(8):
            tops = [cross(state_ref[0, t, a, o], state_ref[1, t, a, o], 64) for t in range(2)]
            sides = [cross(tops[0][b], tops[1][b], 32)[0] for b in range(2)]
            for k, side in enumerate(in_order(own, *sides)):
                made[k].append(side)
            for t in range(2):
                made[2 + t].append(cross(*tops[t], 32)[1])
        for k, blocks in enumerate(made):
            for low, block in enumerate(turned(blocks)):
                for high in range(2):
                    p = 8 * high + low
                    if k < 2:
                        outs[k][a, p] = block[high]
                    else:
                        outs[2][8 * (k - 2) + a, p] = block[high]
        return carry

    lax.fori_loop(0, 8, some, 0, unroll=2)


def pack(state):
    vmem = pl.BlockSpec(memory_space=pltpu.VMEM)
    return pl.pallas_call(
        pack_kernel,
        out_shape=[jax.ShapeDtypeStruct(shape, F32) for shape in (PART, PART, STATE)],
        in_specs=[vmem],
        out_specs=[vmem] * 3,
        cost_estimate=pl.CostEstimate(flops=0, bytes_accessed=4 << 20, transcendentals=0),
        compiler_params=pltpu.CompilerParams(vmem_limit_bytes=LIMIT),
        name="pack",
    )(state)


def gate_step(first, second, w_high_low, w_high, sign):
    state = jnp.concatenate([first, second], axis=1)
    turned = jnp.concatenate(
        [pltpu.roll(first, HALF, 1) * sign, pltpu.roll(second, HALF, 1) * sign], axis=1
    )
    high, low = split(jnp.concatenate([state, turned], axis=0))
    both = jnp.dot(w_high_low, high, preferred_element_type=F32)
    small = jnp.dot(w_high, low, preferred_element_type=F32)
    return both[:GD] + (both[GD:] + small)


def segment_kernel(source, target, n_in, unroll, *refs):
    w_ref = refs[0]
    ins = refs[1 : 1 + n_in]
    outs = refs[1 + n_in : -2]
    one, two = refs[-2:]
    lane = lax.broadcasted_iota(jnp.int32, (1, GD), 1)
    sign = jnp.where(lane < HALF, -1.0, 1.0)
    upper = lax.broadcasted_iota(jnp.int32, (1, 8, GD), 1) >= 4

    own = lax.axis_index("row") >> 4 == 1

    def load_start(i):
        blocks = []
        for p in (2 * i, 2 * i + 1):
            sides = in_order(own, ins[0][:, p].reshape(HALF, GD), ins[1][:, p].reshape(HALF, GD))
            blocks.append(jnp.concatenate(cross(*sides, 32), axis=0))
        return blocks

    def load_whole(i):
        return [ins[0][:, p].reshape(GD, GD) for p in (2 * i, 2 * i + 1)]

    def load_join(i):
        blocks = []
        for p in (2 * i, 2 * i + 1):
            sides = in_order(own, ins[0][:, p].reshape(HALF, GD), ins[1][:, p].reshape(HALF, GD))
            blocks.append(jnp.concatenate(sides, axis=0))
        return blocks

    def load_turn(i):
        blocks = []
        for p in (2 * i, 2 * i + 1):
            sides = ins[0][:8, p].reshape(HALF, GD), ins[0][8:, p].reshape(HALF, GD)
            blocks.append(jnp.concatenate(cross(*sides, 32), axis=0))
        return blocks

    def load_pair(i):
        return [
            jnp.concatenate(
                [ins[0][:, p].reshape(HALF, GD), ins[1][:, p].reshape(HALF, GD)], axis=0
            )
            for p in (2 * i, 2 * i + 1)
        ]

    def load_remap(i):
        def half(c):
            return jnp.concatenate([ins[z][c, :, i] for z in range(4)], axis=0)

        near, far = half(0), half(1)
        even = jnp.where(upper, pltpu.roll(far, 4, 1), near)
        odd = jnp.where(upper, far, pltpu.roll(near, 4, 1))
        z_own = lax.axis_index("row") >> 3
        blocks = []
        for rows in (even, odd):
            near_rows = [], []
            for z in range(2):
                swapped = ((z_own - z) & 3) >= 2
                sides = in_order(swapped, rows[4 * z : 4 * z + 4], rows[4 * z + 8 : 4 * z + 12])
                for k, side in enumerate(cross(*sides, 32)):
                    near_rows[k].append(side)
            blocks.append(jnp.concatenate(near_rows[0] + near_rows[1], axis=0).reshape(GD, GD))
        return blocks

    load = {
        "start": load_start,
        "pair": load_pair,
        "turn": load_turn,
        "whole": load_whole,
        "join": load_join,
        "remap": load_remap,
    }[source[0]]

    def top_first(i, carry):
        first, second = load(i)
        result = gate_step(first, second, w_ref[0], w_ref[0, :GD], sign)
        one[:, 2 * i] = result[:, :GD].reshape(16, 8, GD)
        one[:, 2 * i + 1] = result[:, GD:].reshape(16, 8, GD)
        return carry

    def mid(i, carry):
        first = one[2 * i].reshape(GD, GD)
        second = one[2 * i + 1].reshape(GD, GD)
        result = gate_step(first, second, w_ref[1], w_ref[1, :GD], sign)
        two[2 * i] = result[:, :GD].reshape(16, 8, GD)
        two[2 * i + 1] = result[:, GD:].reshape(16, 8, GD)
        return carry

    def top_last(i, carry):
        first = two[:, 2 * i].reshape(GD, GD)
        second = two[:, 2 * i + 1].reshape(GD, GD)
        result = gate_step(first, second, w_ref[2], w_ref[2, :GD], sign)
        pieces = (result[:, :GD], result[:, GD:])
        if target == "pair":
            for p, piece in zip((2 * i, 2 * i + 1), pieces):
                outs[0][:, p] = piece[:HALF].reshape(8, 8, GD)
                outs[1][:, p] = piece[HALF:].reshape(8, 8, GD)
        elif target == "leave":
            for p, piece in zip((2 * i, 2 * i + 1), pieces):
                sides = in_order(own, *cross(piece[:HALF], piece[HALF:], 32))
                for out, side in zip(outs, sides):
                    out[:, p] = side.reshape(8, 8, GD)
        elif target == "remap":
            even, odd = (piece.reshape(16, 8, GD) for piece in pieces)
            outs[0][:, i] = jnp.where(upper, pltpu.roll(odd, 4, 1), even)
            outs[1][:, i] = jnp.where(upper, odd, pltpu.roll(even, 4, 1))
        else:
            held = outs[0] if target == "plain" else one
            for p, piece in zip((2 * i, 2 * i + 1), pieces):
                held[:, p] = piece.reshape(16, 8, GD)
        return carry

    def low_gate(i, carry):
        low_ref = ins[-1]
        rows = one[pl.ds(4 * i, 4)].reshape(512, GD)
        pair = jnp.concatenate(split(rows), axis=1)
        done = jnp.dot(pair, low_ref[source[1], 0], preferred_element_type=F32) + jnp.dot(
            pair, low_ref[source[1], 1], preferred_element_type=F32
        )
        if target == "share":
            outs[0][i] = done
            return carry
        done = done + ins[-2][i]
        for c in range(2):
            part = done[:, GD * c : GD * (c + 1)].reshape(4, 2, 8, 8, GD)
            blocks = [part[:, :, k].reshape(8, 8, GD) for k in range(8)]
            for o, block in enumerate(turned(blocks)):
                outs[0][c, pl.ds(4 * i, 4), o] = block.reshape(4, 2, 8, GD)
        return carry

    for step in (top_first, mid, top_last):
        lax.fori_loop(0, 8, step, 0, unroll=unroll)
    if target in ("share", "low"):
        lax.fori_loop(0, 4, low_gate, 0, unroll=4 if unroll == 8 else 1)


def run_segment(source, target, w, ins, extra=(), unroll=8):
    if target in ("pair", "leave"):
        out_shape = [jax.ShapeDtypeStruct(PART, F32)] * 2
    elif target == "remap":
        out_shape = [jax.ShapeDtypeStruct((16, 8, 8, 128), F32)] * 2
    elif target == "plain":
        out_shape = [jax.ShapeDtypeStruct(STATE, F32)]
    elif target == "share":
        out_shape = [jax.ShapeDtypeStruct((4, 512, 256), F32)]
    else:
        out_shape = [jax.ShapeDtypeStruct((2, 16, 8, 2, 8, 128), F32)]
    args = list(ins) + list(extra)
    vmem = pl.BlockSpec(memory_space=pltpu.VMEM)
    return pl.pallas_call(
        functools.partial(segment_kernel, source, target, len(args), unroll),
        out_shape=out_shape,
        in_specs=[vmem] * (1 + len(args)),
        out_specs=[vmem] * len(out_shape),
        scratch_shapes=[pltpu.VMEM(STATE, F32)] * 2,
        cost_estimate=pl.CostEstimate(
            flops=3 * 3 * 2 * 128 * 256 * 2048, bytes_accessed=3 << 20, transcendentals=0
        ),
        compiler_params=pltpu.CompilerParams(vmem_limit_bytes=LIMIT),
    )(w, *args)


def regroup_kernel(order, *refs):
    ins, outs = refs[:-4], refs[-4:]
    for j in range(4):
        for k in range(4):
            for c in range(2):
                if order == "swap":
                    outs[j][c, k] = ins[k][c, j]
                else:
                    outs[j][c, k] = ins[c][4 * j + k]


def regroup(order, blocks):
    vmem = pl.BlockSpec(memory_space=pltpu.VMEM)
    return pl.pallas_call(
        functools.partial(regroup_kernel, order),
        out_shape=[jax.ShapeDtypeStruct((2, 4, 8, 8, 128), F32)] * 4,
        in_specs=[vmem] * len(blocks),
        out_specs=[vmem] * 4,
        cost_estimate=pl.CostEstimate(flops=0, bytes_accessed=2 << 20, transcendentals=0),
        compiler_params=pltpu.CompilerParams(vmem_limit_bytes=LIMIT),
    )(*blocks)


def flip(value, axis, mask):
    return lax.ppermute(value, axis, [(s, s ^ mask) for s in range(lax.axis_size(axis))])


def shift_row(value, z, x, c):
    pairs = []
    for s in range(32):
        to = ((((s >> 3) + z) & 3) << 3) | ((((s >> 1) + x) & 3) << 1) | ((s & 1) ^ c)
        pairs.append((s, to))
    return lax.ppermute(value, "row", pairs)


def shift_x(blocks):
    moved = [blocks[0]]
    for x in range(1, 4):
        moved.append(shift_row(blocks[x], 0, x, 0))
    return moved


def shift_z(blocks):
    moved = [blocks[0]]
    for z in range(1, 4):
        moved.append(shift_row(blocks[z], z, 0, 0))
    return moved


def circuit(amplitudes, gate_matrices, permutation):
    state = amplitudes.reshape(2, 2, 8, 8, 2, 8, 128)
    mid = ("mid", "mid")
    kinds = (
        ((None, None), mid, ("xor2", None)),
        ((None, "xor2"), mid, (None, None)),
        ((None, None), mid, ("dest", None)),
        ((None, "src"), mid, ("xor4", None)),
        ((None, "xor4"), mid, (None, None)),
    )
    w = [
        weights(gate_matrices, seg, kinds[seg], permutation if seg == 3 else None)
        for seg in range(5)
    ]
    low = low_weights(gate_matrices)
    halves = (0, 1)
    kept, sent, got = {}, {}, {}
    stays, leaves, whole = pack(state)
    firsts = ("start",), [stays, flip(leaves, "row", 16)]
    for h in halves:
        source, ins = firsts if h == 0 else (("whole",), [whole])
        kept[h], out = run_segment(source, "pair", w[0], ins)
        sent[h] = flip(out, "row", 1)
        pair = [kept[h], sent[h]]
        if h == 0:
            pair = run_segment(("pair",), "plain", w[1], pair)
        else:
            stays, leaves = run_segment(("pair",), "leave", w[1], pair)
            pair = [stays, flip(leaves, "row", 16)]
        near, far = run_segment(("turn", "join")[h : h + 1], "remap", w[2], pair)
        pair = [near, flip(far, "row", 1)]
        moved = shift_x(regroup("by_x", pair))
        got[h] = shift_z(regroup("swap", moved))
    for h in halves:
        kept[h], out = run_segment(("remap",), "pair", w[3], got[h])
        sent[h] = flip(out, "col", 4)
    (share,) = run_segment(("pair", 0), "share", w[4], [kept[0], sent[0]], [low], unroll=4)
    (out,) = run_segment(("pair", 1), "low", w[4], [kept[1], sent[1]], [share, low])
    return out.reshape(amplitudes.shape)


def solution(mesh):
    placed = (P(None, "row", "col", None), P(), P())
    return jax.shard_map(
        circuit, mesh=mesh, in_specs=placed, out_specs=P(None, "row", "col", None), check_vma=False
    )
```

```python
import functools

import jax
import jax.numpy as jnp
from jax import lax
from jax.experimental import pallas as pl
from jax.experimental.pallas import tpu as pltpu
from jax.sharding import PartitionSpec as P


F32 = jnp.float32
BF16 = jnp.bfloat16
GD = 128
HALF = 64
LIMIT = 16 << 20
STATE = (16, 16, 8, 128)
PART = (8, 16, 8, 128)


def split(value):
    high = value.astype(BF16)
    return high, (value - high.astype(F32)).astype(BF16)


def onehot(kind, perm_ref):
    row = lax.axis_index("row")
    col = lax.axis_index("col")
    new = lax.broadcasted_iota(jnp.int32, (GD, GD), 0)
    old = lax.broadcasted_iota(jnp.int32, (GD, GD), 1)
    z_own, x_own, c_own = row >> 3, (row >> 1) & 3, row & 1
    rest, core, block = new & 3, (new >> 2) & 1, new >> 3
    if kind == "mid":
        want = ((new & 7) << 4) | (new >> 3)
    elif kind[:3] == "xor":
        want = new ^ ({"xor2": c_own, "xor4": col >> 2}[kind] << 6)
    elif kind == "dest":
        x = ((block >> 2) + x_own) & 3
        z = ((block & 3) + z_own) & 3
        want = (((((z << 2) | x) << 1) | (core ^ c_own)) << 2) | rest
    else:
        z = ((block >> 3) << 1) | ((z_own - (block >> 2)) & 1)
        x = (x_own - (block & 3)) & 3
        want = (((((z << 2) | x) << 1) | (core ^ c_own)) << 2) | rest
        state = lax.broadcasted_iota(jnp.int32, (1, GD), 1)
        moved = state & 3
        for t in range(32):
            moved += jnp.where(state >> 2 == t, perm_ref[t] * 4, 0)
        old = jnp.broadcast_to(moved, (GD, GD))
    return jnp.where(want == old, 1.0, 0.0).astype(BF16)


def weight_kernel(kinds, n_prefetch, *refs):
    perm_ref = refs[0] if n_prefetch else None
    gates_ref, out_ref = refs[n_prefetch], refs[-1]
    made = {}
    for number, (rows, cols) in enumerate(kinds):
        for kind in (rows, cols):
            if kind is not None and kind not in made:
                made[kind] = onehot(kind, perm_ref)
        slot = (0, 1, 3)[number]
        real_high, real_low = split(gates_ref[0, slot, 0])
        imag_high, imag_low = split(gates_ref[0, slot, 1])
        wide = jnp.concatenate([real_high, imag_high, real_low, imag_low], axis=1)
        if rows is not None:
            wide = jnp.dot(made[rows], wide, preferred_element_type=F32).astype(BF16)
        parts = [wide[:, GD * i : GD * (i + 1)] for i in range(4)]
        if cols is not None:
            tall = lax.dot_general(
                jnp.concatenate(parts, axis=0),
                made[cols],
                (((1,), (1,)), ((), ())),
                preferred_element_type=F32,
            ).astype(BF16)
            parts = [tall[GD * i : GD * (i + 1)] for i in range(4)]
        out_ref[number, 0:GD, 0:GD] = parts[0]
        out_ref[number, 0:GD, GD:] = parts[1]
        out_ref[number, GD:, 0:GD] = parts[2]
        out_ref[number, GD:, GD:] = parts[3]


def weights(gate_matrices, seg, kinds, permutation):
    prefetch = () if permutation is None else (permutation,)
    block = seg
    if seg == 0:
        block, gate_matrices = 0, gate_matrices[:1]
    return pl.pallas_call(
        functools.partial(weight_kernel, kinds, len(prefetch)),
        out_shape=jax.ShapeDtypeStruct((3, 256, 256), BF16),
        grid_spec=pltpu.PrefetchScalarGridSpec(
            num_scalar_prefetch=len(prefetch),
            grid=(1,),
            in_specs=[pl.BlockSpec((1, 4, 2, GD, GD), lambda i, *_: (block, 0, 0, 0, 0))],
            out_specs=pl.BlockSpec(memory_space=pltpu.VMEM),
        ),
        cost_estimate=pl.CostEstimate(
            flops=3 * 2 * 640 * 128 * 512, bytes_accessed=1 << 20, transcendentals=0
        ),
        compiler_params=pltpu.CompilerParams(vmem_limit_bytes=LIMIT),
    )(*prefetch, gate_matrices)


def low_kernel(gates_ref, out_ref, total_ref):
    seg = pl.program_id(0)
    real, imag = gates_ref[0, 0, 0], gates_ref[0, 0, 1]
    form = jnp.concatenate(
        [jnp.concatenate([real, -imag], axis=1), jnp.concatenate([imag, real], axis=1)], axis=0
    )

    @pl.when(seg == 0)
    def _():
        new = lax.broadcasted_iota(jnp.int32, (256, 256), 0)
        old = lax.broadcasted_iota(jnp.int32, (256, 256), 1)
        want = (((new >> 6) & 1) << 7) | (((new >> 5) & 1) << 6) | ((new >> 7) << 5) | (new & 31)
        total_ref[...] = jnp.where(want == old, 1.0, 0.0)

    high, low = split(total_ref[...])
    form_high, form_low = split(form)

    def times(left, right):
        return lax.dot_general(
            left, right, (((1,), (1,)), ((), ())), preferred_element_type=F32
        )

    total = times(high, form_high) + (times(high, form_low) + times(low, form_high))
    total_ref[...] = total
    for k, piece in enumerate(split(total)):
        for h in range(2):
            rows = piece[GD * h : GD * (h + 1)]
            out_ref[h, k, 0:GD] = rows
            out_ref[h, k, GD:] = rows


def low_weights(gate_matrices):
    return pl.pallas_call(
        low_kernel,
        out_shape=jax.ShapeDtypeStruct((2, 2, 256, 256), BF16),
        grid=(gate_matrices.shape[0],),
        in_specs=[pl.BlockSpec((1, 1, 2, GD, GD), lambda i: (i, 2, 0, 0, 0))],
        out_specs=pl.BlockSpec(memory_space=pltpu.VMEM),
        scratch_shapes=[pltpu.VMEM((256, 256), F32)],
        cost_estimate=pl.CostEstimate(
            flops=5 * 3 * 2 * 256**3, bytes_accessed=1 << 20, transcendentals=0
        ),
        compiler_params=pltpu.CompilerParams(vmem_limit_bytes=LIMIT),
        name="low_weights",
    )(gate_matrices)


def cross(first, second, step):
    axis = first.ndim - 1
    lane = lax.broadcasted_iota(jnp.int32, (1,) * axis + (GD,), axis)
    off = (lane & step) == 0
    return (
        jnp.where(off, first, pltpu.roll(second, step, axis)),
        jnp.where(off, pltpu.roll(first, GD - step, axis), second),
    )


def in_order(swapped, first, second):
    return jnp.where(swapped, second, first), jnp.where(swapped, first, second)


def turned(blocks):
    sub = lax.broadcasted_iota(jnp.int32, (1, 8, 1), 1)
    for step in (1, 2, 4):
        off = (sub & step) == 0
        made = [None] * 8
        for k in range(8):
            if k & step:
                continue
            first, second = blocks[k], blocks[k + step]
            made[k] = jnp.where(off, first, pltpu.roll(second, step, 1))
            made[k + step] = jnp.where(off, pltpu.roll(first, 8 - step, 1), second)
        blocks = made
    return blocks


def pack_kernel(state_ref, *outs):
    own = lax.axis_index("row") >> 4 == 1

    def some(p, carry):
        tops = []
        for top in range(2):
            rows = [state_ref[c, pl.ds(1024 * top + p, HALF, stride=16), :] for c in range(2)]
            tops.append(cross(rows[0], rows[1], 64))
        sides = [cross(tops[0][b], tops[1][b], 32)[0] for b in range(2)]
        for out, side in zip(outs[:2], in_order(own, *sides)):
            out[:, p] = side.reshape(8, 8, GD)
        for top in range(2):
            outs[2][8 * top : 8 * top + 8, p] = cross(*tops[top], 32)[1].reshape(8, 8, GD)
        return carry

    lax.fori_loop(0, 16, some, 0, unroll=8)


def pack(state):
    vmem = pl.BlockSpec(memory_space=pltpu.VMEM)
    return pl.pallas_call(
        pack_kernel,
        out_shape=[jax.ShapeDtypeStruct(shape, F32) for shape in (PART, PART, STATE)],
        in_specs=[vmem],
        out_specs=[vmem] * 3,
        cost_estimate=pl.CostEstimate(flops=0, bytes_accessed=4 << 20, transcendentals=0),
        compiler_params=pltpu.CompilerParams(vmem_limit_bytes=LIMIT),
        name="pack",
    )(state)


def gate_step(first, second, w_high_low, w_high, sign):
    state = jnp.concatenate([first, second], axis=1)
    turned = jnp.concatenate(
        [pltpu.roll(first, HALF, 1) * sign, pltpu.roll(second, HALF, 1) * sign], axis=1
    )
    high, low = split(jnp.concatenate([state, turned], axis=0))
    both = jnp.dot(w_high_low, high, preferred_element_type=F32)
    small = jnp.dot(w_high, low, preferred_element_type=F32)
    return both[:GD] + (both[GD:] + small)


def segment_kernel(source, target, n_in, unroll, *refs):
    w_ref = refs[0]
    ins = refs[1 : 1 + n_in]
    outs = refs[1 + n_in : -2]
    one, two = refs[-2:]
    lane = lax.broadcasted_iota(jnp.int32, (1, GD), 1)
    sign = jnp.where(lane < HALF, -1.0, 1.0)
    upper = lax.broadcasted_iota(jnp.int32, (1, 8, GD), 1) >= 4

    own = lax.axis_index("row") >> 4 == 1

    def load_start(i):
        blocks = []
        for p in (2 * i, 2 * i + 1):
            sides = in_order(own, ins[0][:, p].reshape(HALF, GD), ins[1][:, p].reshape(HALF, GD))
            blocks.append(jnp.concatenate(cross(*sides, 32), axis=0))
        return blocks

    def load_whole(i):
        return [ins[0][:, p].reshape(GD, GD) for p in (2 * i, 2 * i + 1)]

    def load_join(i):
        blocks = []
        for p in (2 * i, 2 * i + 1):
            sides = in_order(own, ins[0][:, p].reshape(HALF, GD), ins[1][:, p].reshape(HALF, GD))
            blocks.append(jnp.concatenate(sides, axis=0))
        return blocks

    def load_turn(i):
        blocks = []
        for p in (2 * i, 2 * i + 1):
            sides = ins[0][:8, p].reshape(HALF, GD), ins[0][8:, p].reshape(HALF, GD)
            blocks.append(jnp.concatenate(cross(*sides, 32), axis=0))
        return blocks

    def load_pair(i):
        return [
            jnp.concatenate(
                [ins[0][:, p].reshape(HALF, GD), ins[1][:, p].reshape(HALF, GD)], axis=0
            )
            for p in (2 * i, 2 * i + 1)
        ]

    def load_remap(i):
        def half(c):
            if source[1] == "by_x":
                return jnp.stack([ins[x][c, z, i] for z in range(4) for x in range(4)], axis=0)
            return jnp.concatenate([ins[z][c, :, i] for z in range(4)], axis=0)

        near, far = half(0), half(1)
        even = jnp.where(upper, pltpu.roll(far, 4, 1), near)
        odd = jnp.where(upper, far, pltpu.roll(near, 4, 1))
        z_own = lax.axis_index("row") >> 3
        blocks = []
        for rows in (even, odd):
            near_rows = [], []
            for z in range(2):
                swapped = ((z_own - z) & 3) >= 2
                sides = in_order(swapped, rows[4 * z : 4 * z + 4], rows[4 * z + 8 : 4 * z + 12])
                for k, side in enumerate(cross(*sides, 32)):
                    near_rows[k].append(side)
            blocks.append(jnp.concatenate(near_rows[0] + near_rows[1], axis=0).reshape(GD, GD))
        return blocks

    load = {
        "start": load_start,
        "pair": load_pair,
        "turn": load_turn,
        "whole": load_whole,
        "join": load_join,
        "remap": load_remap,
    }[source[0]]

    def top_first(i, carry):
        first, second = load(i)
        result = gate_step(first, second, w_ref[0], w_ref[0, :GD], sign)
        one[:, 2 * i] = result[:, :GD].reshape(16, 8, GD)
        one[:, 2 * i + 1] = result[:, GD:].reshape(16, 8, GD)
        return carry

    def mid(i, carry):
        first = one[2 * i].reshape(GD, GD)
        second = one[2 * i + 1].reshape(GD, GD)
        result = gate_step(first, second, w_ref[1], w_ref[1, :GD], sign)
        two[2 * i] = result[:, :GD].reshape(16, 8, GD)
        two[2 * i + 1] = result[:, GD:].reshape(16, 8, GD)
        return carry

    def top_last(i, carry):
        first = two[:, 2 * i].reshape(GD, GD)
        second = two[:, 2 * i + 1].reshape(GD, GD)
        result = gate_step(first, second, w_ref[2], w_ref[2, :GD], sign)
        pieces = (result[:, :GD], result[:, GD:])
        if target == "pair":
            for p, piece in zip((2 * i, 2 * i + 1), pieces):
                outs[0][:, p] = piece[:HALF].reshape(8, 8, GD)
                outs[1][:, p] = piece[HALF:].reshape(8, 8, GD)
        elif target == "leave":
            for p, piece in zip((2 * i, 2 * i + 1), pieces):
                sides = in_order(own, *cross(piece[:HALF], piece[HALF:], 32))
                for out, side in zip(outs, sides):
                    out[:, p] = side.reshape(8, 8, GD)
        elif target == "remap":
            even, odd = (piece.reshape(16, 8, GD) for piece in pieces)
            outs[0][:, i] = jnp.where(upper, pltpu.roll(odd, 4, 1), even)
            outs[1][:, i] = jnp.where(upper, odd, pltpu.roll(even, 4, 1))
        else:
            held = outs[0] if target == "plain" else one
            for p, piece in zip((2 * i, 2 * i + 1), pieces):
                held[:, p] = piece.reshape(16, 8, GD)
        return carry

    def low_gate(i, carry):
        low_ref = ins[-1]
        rows = one[pl.ds(4 * i, 4)].reshape(512, GD)
        pair = jnp.concatenate(split(rows), axis=1)
        done = jnp.dot(pair, low_ref[source[1], 0], preferred_element_type=F32) + jnp.dot(
            pair, low_ref[source[1], 1], preferred_element_type=F32
        )
        if target == "share":
            outs[0][i] = done
            return carry
        done = done + ins[-2][i]
        for c in range(2):
            part = done[:, GD * c : GD * (c + 1)].reshape(4, 2, 8, 8, GD)
            blocks = [part[:, :, k].reshape(8, 8, GD) for k in range(8)]
            for o, block in enumerate(turned(blocks)):
                outs[0][c, pl.ds(4 * i, 4), o] = block.reshape(4, 2, 8, GD)
        return carry

    for step in (top_first, mid, top_last):
        lax.fori_loop(0, 8, step, 0, unroll=unroll)
    if target in ("share", "low"):
        lax.fori_loop(0, 4, low_gate, 0, unroll=4 if unroll == 8 else 1)


def run_segment(source, target, w, ins, extra=(), unroll=8):
    if target in ("pair", "leave"):
        out_shape = [jax.ShapeDtypeStruct(PART, F32)] * 2
    elif target == "remap":
        out_shape = [jax.ShapeDtypeStruct((16, 8, 8, 128), F32)] * 2
    elif target == "plain":
        out_shape = [jax.ShapeDtypeStruct(STATE, F32)]
    elif target == "share":
        out_shape = [jax.ShapeDtypeStruct((4, 512, 256), F32)]
    else:
        out_shape = [jax.ShapeDtypeStruct((2, 16, 8, 2, 8, 128), F32)]
    args = list(ins) + list(extra)
    vmem = pl.BlockSpec(memory_space=pltpu.VMEM)
    return pl.pallas_call(
        functools.partial(segment_kernel, source, target, len(args), unroll),
        out_shape=out_shape,
        in_specs=[vmem] * (1 + len(args)),
        out_specs=[vmem] * len(out_shape),
        scratch_shapes=[pltpu.VMEM(STATE, F32)] * 2,
        cost_estimate=pl.CostEstimate(
            flops=3 * 3 * 2 * 128 * 256 * 2048, bytes_accessed=3 << 20, transcendentals=0
        ),
        compiler_params=pltpu.CompilerParams(vmem_limit_bytes=LIMIT),
    )(w, *args)


def regroup_kernel(order, *refs):
    ins, outs = refs[:-4], refs[-4:]
    for j in range(4):
        for k in range(4):
            for c in range(2):
                if order == "swap":
                    outs[j][c, k] = ins[k][c, j]
                else:
                    outs[j][c, k] = ins[c][4 * j + k if order == "by_x" else 4 * k + j]


def regroup(order, blocks):
    vmem = pl.BlockSpec(memory_space=pltpu.VMEM)
    return pl.pallas_call(
        functools.partial(regroup_kernel, order),
        out_shape=[jax.ShapeDtypeStruct((2, 4, 8, 8, 128), F32)] * 4,
        in_specs=[vmem] * len(blocks),
        out_specs=[vmem] * 4,
        cost_estimate=pl.CostEstimate(flops=0, bytes_accessed=2 << 20, transcendentals=0),
        compiler_params=pltpu.CompilerParams(vmem_limit_bytes=LIMIT),
    )(*blocks)


def flip(value, axis, mask):
    return lax.ppermute(value, axis, [(s, s ^ mask) for s in range(lax.axis_size(axis))])


def shift_row(value, z, x, c):
    pairs = []
    for s in range(32):
        to = ((((s >> 3) + z) & 3) << 3) | ((((s >> 1) + x) & 3) << 1) | ((s & 1) ^ c)
        pairs.append((s, to))
    return lax.ppermute(value, "row", pairs)


def shift_x(blocks):
    moved = [blocks[0]]
    for x in range(1, 4):
        moved.append(shift_row(blocks[x], 0, x, 0))
    return moved


def shift_z(blocks):
    moved = [blocks[0]]
    for z in range(1, 4):
        moved.append(shift_row(blocks[z], z, 0, 0))
    return moved


def circuit(amplitudes, gate_matrices, permutation):
    state = amplitudes.reshape(2, 2048, 128)
    mid = ("mid", "mid")
    kinds = (
        ((None, None), mid, ("xor2", None)),
        ((None, "xor2"), mid, (None, None)),
        ((None, None), mid, ("dest", None)),
        ((None, "src"), mid, ("xor4", None)),
        ((None, "xor4"), mid, (None, None)),
    )
    w = [
        weights(gate_matrices, seg, kinds[seg], permutation if seg == 3 else None)
        for seg in range(5)
    ]
    low = low_weights(gate_matrices)
    halves = (0, 1)
    kept, sent, got = {}, {}, {}
    stays, leaves, whole = pack(state)
    firsts = ("start",), [stays, flip(leaves, "row", 16)]
    for h in halves:
        source, ins = firsts if h == 0 else (("whole",), [whole])
        kept[h], out = run_segment(source, "pair", w[0], ins)
        sent[h] = flip(out, "row", 1)
        pair = [kept[h], sent[h]]
        if h == 0:
            pair = run_segment(("pair",), "plain", w[1], pair)
        else:
            stays, leaves = run_segment(("pair",), "leave", w[1], pair)
            pair = [stays, flip(leaves, "row", 16)]
        near, far = run_segment(("turn", "join")[h : h + 1], "remap", w[2], pair)
        pair = [near, flip(far, "row", 1)]
        if h == 0:
            moved = shift_z(regroup("by_z", pair))
            got[h] = shift_x(regroup("swap", moved))
        else:
            moved = shift_x(regroup("by_x", pair))
            got[h] = shift_z(regroup("swap", moved))
    for h in halves:
        kept[h], out = run_segment(("remap", ("by_x", "by_z")[h]), "pair", w[3], got[h])
        sent[h] = flip(out, "col", 4)
    (share,) = run_segment(("pair", 0), "share", w[4], [kept[0], sent[0]], [low], unroll=4)
    (out,) = run_segment(("pair", 1), "low", w[4], [kept[1], sent[1]], [share, low])
    return out.reshape(amplitudes.shape)


def solution(mesh):
    placed = (P(None, "row", "col", None), P(), P())
    return jax.shard_map(
        circuit, mesh=mesh, in_specs=placed, out_specs=P(None, "row", "col", None), check_vma=False
    )
```

```python
import functools

import jax
import jax.numpy as jnp
from jax import lax
from jax.experimental import pallas as pl
from jax.experimental.pallas import tpu as pltpu
from jax.sharding import PartitionSpec as P


F32 = jnp.float32
BF16 = jnp.bfloat16
GD = 128
HALF = 64
LIMIT = 16 << 20
STATE = (16, 16, 8, 128)
PART = (8, 16, 8, 128)


def split(value):
    high = value.astype(BF16)
    return high, (value - high.astype(F32)).astype(BF16)


def onehot(kind, perm_ref):
    row = lax.axis_index("row")
    col = lax.axis_index("col")
    new = lax.broadcasted_iota(jnp.int32, (GD, GD), 0)
    old = lax.broadcasted_iota(jnp.int32, (GD, GD), 1)
    z_own, x_own, c_own = row >> 3, (row >> 1) & 3, row & 1
    rest, core, block = new & 3, (new >> 2) & 1, new >> 3
    if kind == "mid":
        want = ((new & 7) << 4) | (new >> 3)
    elif kind[:3] == "xor":
        want = new ^ ({"xor2": c_own, "xor4": col >> 2}[kind] << 6)
    elif kind == "dest":
        x = ((block >> 2) + x_own) & 3
        z = ((block & 3) + z_own) & 3
        want = (((((z << 2) | x) << 1) | (core ^ c_own)) << 2) | rest
    else:
        z = ((block >> 3) << 1) | ((z_own - (block >> 2)) & 1)
        x = (x_own - (block & 3)) & 3
        want = (((((z << 2) | x) << 1) | (core ^ c_own)) << 2) | rest
        state = lax.broadcasted_iota(jnp.int32, (1, GD), 1)
        moved = state & 3
        for t in range(32):
            moved += jnp.where(state >> 2 == t, perm_ref[t] * 4, 0)
        old = jnp.broadcast_to(moved, (GD, GD))
    return jnp.where(want == old, 1.0, 0.0).astype(BF16)


def weight_kernel(kinds, n_prefetch, *refs):
    perm_ref = refs[0] if n_prefetch else None
    gates_ref, out_ref = refs[n_prefetch], refs[-1]
    made = {}
    for number, (rows, cols) in enumerate(kinds):
        for kind in (rows, cols):
            if kind is not None and kind not in made:
                made[kind] = onehot(kind, perm_ref)
        slot = (0, 1, 3)[number]
        real_high, real_low = split(gates_ref[0, slot, 0])
        imag_high, imag_low = split(gates_ref[0, slot, 1])
        wide = jnp.concatenate([real_high, imag_high, real_low, imag_low], axis=1)
        if rows is not None:
            wide = jnp.dot(made[rows], wide, preferred_element_type=F32).astype(BF16)
        parts = [wide[:, GD * i : GD * (i + 1)] for i in range(4)]
        if cols is not None:
            tall = lax.dot_general(
                jnp.concatenate(parts, axis=0),
                made[cols],
                (((1,), (1,)), ((), ())),
                preferred_element_type=F32,
            ).astype(BF16)
            parts = [tall[GD * i : GD * (i + 1)] for i in range(4)]
        out_ref[number, 0:GD, 0:GD] = parts[0]
        out_ref[number, 0:GD, GD:] = parts[1]
        out_ref[number, GD:, 0:GD] = parts[2]
        out_ref[number, GD:, GD:] = parts[3]


def weights(gate_matrices, seg, kinds, permutation):
    prefetch = () if permutation is None else (permutation,)
    block = seg
    if seg == 0:
        block, gate_matrices = 0, gate_matrices[:1]
    return pl.pallas_call(
        functools.partial(weight_kernel, kinds, len(prefetch)),
        out_shape=jax.ShapeDtypeStruct((3, 256, 256), BF16),
        grid_spec=pltpu.PrefetchScalarGridSpec(
            num_scalar_prefetch=len(prefetch),
            grid=(1,),
            in_specs=[pl.BlockSpec((1, 4, 2, GD, GD), lambda i, *_: (block, 0, 0, 0, 0))],
            out_specs=pl.BlockSpec(memory_space=pltpu.VMEM),
        ),
        cost_estimate=pl.CostEstimate(
            flops=3 * 2 * 640 * 128 * 512, bytes_accessed=1 << 20, transcendentals=0
        ),
        compiler_params=pltpu.CompilerParams(vmem_limit_bytes=LIMIT),
    )(*prefetch, gate_matrices)


def low_kernel(gates_ref, out_ref, total_ref):
    seg = pl.program_id(0)
    real, imag = gates_ref[0, 0, 0], gates_ref[0, 0, 1]
    form = jnp.concatenate(
        [jnp.concatenate([real, -imag], axis=1), jnp.concatenate([imag, real], axis=1)], axis=0
    )

    @pl.when(seg == 0)
    def _():
        new = lax.broadcasted_iota(jnp.int32, (256, 256), 0)
        old = lax.broadcasted_iota(jnp.int32, (256, 256), 1)
        want = (((new >> 6) & 1) << 7) | (((new >> 5) & 1) << 6) | ((new >> 7) << 5) | (new & 31)
        total_ref[...] = jnp.where(want == old, 1.0, 0.0)

    high, low = split(total_ref[...])
    form_high, form_low = split(form)

    def times(left, right):
        return lax.dot_general(
            left, right, (((1,), (1,)), ((), ())), preferred_element_type=F32
        )

    total = times(high, form_high) + (times(high, form_low) + times(low, form_high))
    total_ref[...] = total
    for k, piece in enumerate(split(total)):
        for h in range(2):
            rows = piece[GD * h : GD * (h + 1)]
            out_ref[h, k, 0:GD] = rows
            out_ref[h, k, GD:] = rows


def low_weights(gate_matrices):
    return pl.pallas_call(
        low_kernel,
        out_shape=jax.ShapeDtypeStruct((2, 2, 256, 256), BF16),
        grid=(gate_matrices.shape[0],),
        in_specs=[pl.BlockSpec((1, 1, 2, GD, GD), lambda i: (i, 2, 0, 0, 0))],
        out_specs=pl.BlockSpec(memory_space=pltpu.VMEM),
        scratch_shapes=[pltpu.VMEM((256, 256), F32)],
        cost_estimate=pl.CostEstimate(
            flops=5 * 3 * 2 * 256**3, bytes_accessed=1 << 20, transcendentals=0
        ),
        compiler_params=pltpu.CompilerParams(vmem_limit_bytes=LIMIT),
        name="low_weights",
    )(gate_matrices)


def cross(first, second, step):
    axis = first.ndim - 1
    lane = lax.broadcasted_iota(jnp.int32, (1,) * axis + (GD,), axis)
    off = (lane & step) == 0
    return (
        jnp.where(off, first, pltpu.roll(second, step, axis)),
        jnp.where(off, pltpu.roll(first, GD - step, axis), second),
    )


def in_order(swapped, first, second):
    return jnp.where(swapped, second, first), jnp.where(swapped, first, second)


def turned(blocks):
    sub = lax.broadcasted_iota(jnp.int32, (1, 8, 1), 1)
    for step in (1, 2, 4):
        off = (sub & step) == 0
        made = [None] * 8
        for k in range(8):
            if k & step:
                continue
            first, second = blocks[k], blocks[k + step]
            made[k] = jnp.where(off, first, pltpu.roll(second, step, 1))
            made[k + step] = jnp.where(off, pltpu.roll(first, 8 - step, 1), second)
        blocks = made
    return blocks


def pack_kernel(state_ref, *outs):
    own = lax.axis_index("row") >> 4 == 1

    def some(i, carry):
        rows = pl.ds(GD * i, GD)
        tops = [cross(state_ref[0, t, rows], state_ref[1, t, rows], 64) for t in range(2)]
        sides = [cross(tops[0][b], tops[1][b], 32)[0] for b in range(2)]
        for out, side in zip(outs[:2], in_order(own, *sides)):
            out[rows] = side
        for t in range(2):
            outs[2][t, rows] = cross(*tops[t], 32)[1]
        return carry

    lax.fori_loop(0, 8, some, 0, unroll=4)


def pack(state):
    vmem = pl.BlockSpec(memory_space=pltpu.VMEM)
    return pl.pallas_call(
        pack_kernel,
        out_shape=[
            jax.ShapeDtypeStruct(shape, F32)
            for shape in ((1024, 128), (1024, 128), (2, 1024, 128))
        ],
        in_specs=[vmem],
        out_specs=[vmem] * 3,
        cost_estimate=pl.CostEstimate(flops=0, bytes_accessed=4 << 20, transcendentals=0),
        compiler_params=pltpu.CompilerParams(vmem_limit_bytes=LIMIT),
        name="pack",
    )(state)


def gate_step(first, second, w_high_low, w_high, sign):
    state = jnp.concatenate([first, second], axis=1)
    turned = jnp.concatenate(
        [pltpu.roll(first, HALF, 1) * sign, pltpu.roll(second, HALF, 1) * sign], axis=1
    )
    high, low = split(jnp.concatenate([state, turned], axis=0))
    both = jnp.dot(w_high_low, high, preferred_element_type=F32)
    small = jnp.dot(w_high, low, preferred_element_type=F32)
    return both[:GD] + (both[GD:] + small)


def segment_kernel(source, target, n_in, unroll, *refs):
    w_ref = refs[0]
    ins = refs[1 : 1 + n_in]
    outs = refs[1 + n_in : -2]
    one, two = refs[-2:]
    lane = lax.broadcasted_iota(jnp.int32, (1, GD), 1)
    sign = jnp.where(lane < HALF, -1.0, 1.0)
    upper = lax.broadcasted_iota(jnp.int32, (1, 8, GD), 1) >= 4

    own = lax.axis_index("row") >> 4 == 1

    def load_start(i):
        blocks = []
        for p in (2 * i, 2 * i + 1):
            rows = pl.ds(p, HALF, stride=16)
            sides = in_order(own, ins[0][rows, :], ins[1][rows, :])
            blocks.append(jnp.concatenate(cross(*sides, 32), axis=0))
        return blocks

    def load_whole(i):
        blocks = []
        for p in (2 * i, 2 * i + 1):
            rows = pl.ds(p, HALF, stride=16)
            blocks.append(jnp.concatenate([ins[0][0, rows, :], ins[0][1, rows, :]], axis=0))
        return blocks

    def load_join(i):
        blocks = []
        for p in (2 * i, 2 * i + 1):
            sides = in_order(own, ins[0][:, p].reshape(HALF, GD), ins[1][:, p].reshape(HALF, GD))
            blocks.append(jnp.concatenate(sides, axis=0))
        return blocks

    def load_turn(i):
        blocks = []
        for p in (2 * i, 2 * i + 1):
            sides = ins[0][:8, p].reshape(HALF, GD), ins[0][8:, p].reshape(HALF, GD)
            blocks.append(jnp.concatenate(cross(*sides, 32), axis=0))
        return blocks

    def load_pair(i):
        return [
            jnp.concatenate(
                [ins[0][:, p].reshape(HALF, GD), ins[1][:, p].reshape(HALF, GD)], axis=0
            )
            for p in (2 * i, 2 * i + 1)
        ]

    def load_remap(i):
        def half(c):
            if source[1] == "by_x":
                return jnp.stack([ins[x][c, z, i] for z in range(4) for x in range(4)], axis=0)
            return jnp.concatenate([ins[z][c, :, i] for z in range(4)], axis=0)

        near, far = half(0), half(1)
        even = jnp.where(upper, pltpu.roll(far, 4, 1), near)
        odd = jnp.where(upper, far, pltpu.roll(near, 4, 1))
        z_own = lax.axis_index("row") >> 3
        blocks = []
        for rows in (even, odd):
            near_rows = [], []
            for z in range(2):
                swapped = ((z_own - z) & 3) >= 2
                sides = in_order(swapped, rows[4 * z : 4 * z + 4], rows[4 * z + 8 : 4 * z + 12])
                for k, side in enumerate(cross(*sides, 32)):
                    near_rows[k].append(side)
            blocks.append(jnp.concatenate(near_rows[0] + near_rows[1], axis=0).reshape(GD, GD))
        return blocks

    load = {
        "start": load_start,
        "pair": load_pair,
        "turn": load_turn,
        "whole": load_whole,
        "join": load_join,
        "remap": load_remap,
    }[source[0]]

    def top_first(i, carry):
        first, second = load(i)
        result = gate_step(first, second, w_ref[0], w_ref[0, :GD], sign)
        one[:, 2 * i] = result[:, :GD].reshape(16, 8, GD)
        one[:, 2 * i + 1] = result[:, GD:].reshape(16, 8, GD)
        return carry

    def mid(i, carry):
        first = one[2 * i].reshape(GD, GD)
        second = one[2 * i + 1].reshape(GD, GD)
        result = gate_step(first, second, w_ref[1], w_ref[1, :GD], sign)
        two[2 * i] = result[:, :GD].reshape(16, 8, GD)
        two[2 * i + 1] = result[:, GD:].reshape(16, 8, GD)
        return carry

    def top_last(i, carry):
        first = two[:, 2 * i].reshape(GD, GD)
        second = two[:, 2 * i + 1].reshape(GD, GD)
        result = gate_step(first, second, w_ref[2], w_ref[2, :GD], sign)
        pieces = (result[:, :GD], result[:, GD:])
        if target == "pair":
            for p, piece in zip((2 * i, 2 * i + 1), pieces):
                outs[0][:, p] = piece[:HALF].reshape(8, 8, GD)
                outs[1][:, p] = piece[HALF:].reshape(8, 8, GD)
        elif target == "leave":
            for p, piece in zip((2 * i, 2 * i + 1), pieces):
                sides = in_order(own, *cross(piece[:HALF], piece[HALF:], 32))
                for out, side in zip(outs, sides):
                    out[:, p] = side.reshape(8, 8, GD)
        elif target == "remap":
            even, odd = (piece.reshape(16, 8, GD) for piece in pieces)
            outs[0][:, i] = jnp.where(upper, pltpu.roll(odd, 4, 1), even)
            outs[1][:, i] = jnp.where(upper, odd, pltpu.roll(even, 4, 1))
        else:
            held = outs[0] if target == "plain" else one
            for p, piece in zip((2 * i, 2 * i + 1), pieces):
                held[:, p] = piece.reshape(16, 8, GD)
        return carry

    def low_gate(i, carry):
        low_ref = ins[-1]
        rows = one[pl.ds(4 * i, 4)].reshape(512, GD)
        pair = jnp.concatenate(split(rows), axis=1)
        done = jnp.dot(pair, low_ref[source[1], 0], preferred_element_type=F32) + jnp.dot(
            pair, low_ref[source[1], 1], preferred_element_type=F32
        )
        if target == "share":
            outs[0][i] = done
            return carry
        done = done + ins[-2][i]
        for c in range(2):
            part = done[:, GD * c : GD * (c + 1)].reshape(4, 2, 8, 8, GD)
            blocks = [part[:, :, k].reshape(8, 8, GD) for k in range(8)]
            for o, block in enumerate(turned(blocks)):
                outs[0][c, pl.ds(4 * i, 4), o] = block.reshape(4, 2, 8, GD)
        return carry

    for step in (top_first, mid, top_last):
        lax.fori_loop(0, 8, step, 0, unroll=unroll)
    if target in ("share", "low"):
        lax.fori_loop(0, 4, low_gate, 0, unroll=4 if unroll == 8 else 1)


def run_segment(source, target, w, ins, extra=(), unroll=8):
    if target in ("pair", "leave"):
        out_shape = [jax.ShapeDtypeStruct(PART, F32)] * 2
    elif target == "remap":
        out_shape = [jax.ShapeDtypeStruct((16, 8, 8, 128), F32)] * 2
    elif target == "plain":
        out_shape = [jax.ShapeDtypeStruct(STATE, F32)]
    elif target == "share":
        out_shape = [jax.ShapeDtypeStruct((4, 512, 256), F32)]
    else:
        out_shape = [jax.ShapeDtypeStruct((2, 16, 8, 2, 8, 128), F32)]
    args = list(ins) + list(extra)
    vmem = pl.BlockSpec(memory_space=pltpu.VMEM)
    return pl.pallas_call(
        functools.partial(segment_kernel, source, target, len(args), unroll),
        out_shape=out_shape,
        in_specs=[vmem] * (1 + len(args)),
        out_specs=[vmem] * len(out_shape),
        scratch_shapes=[pltpu.VMEM(STATE, F32)] * 2,
        cost_estimate=pl.CostEstimate(
            flops=3 * 3 * 2 * 128 * 256 * 2048, bytes_accessed=3 << 20, transcendentals=0
        ),
        compiler_params=pltpu.CompilerParams(vmem_limit_bytes=LIMIT),
    )(w, *args)


def regroup_kernel(order, *refs):
    ins, outs = refs[:-4], refs[-4:]
    for j in range(4):
        for k in range(4):
            for c in range(2):
                if order == "swap":
                    outs[j][c, k] = ins[k][c, j]
                else:
                    outs[j][c, k] = ins[c][4 * j + k if order == "by_x" else 4 * k + j]


def regroup(order, blocks):
    vmem = pl.BlockSpec(memory_space=pltpu.VMEM)
    return pl.pallas_call(
        functools.partial(regroup_kernel, order),
        out_shape=[jax.ShapeDtypeStruct((2, 4, 8, 8, 128), F32)] * 4,
        in_specs=[vmem] * len(blocks),
        out_specs=[vmem] * 4,
        cost_estimate=pl.CostEstimate(flops=0, bytes_accessed=2 << 20, transcendentals=0),
        compiler_params=pltpu.CompilerParams(vmem_limit_bytes=LIMIT),
    )(*blocks)


def flip(value, axis, mask):
    return lax.ppermute(value, axis, [(s, s ^ mask) for s in range(lax.axis_size(axis))])


def shift_row(value, z, x, c):
    pairs = []
    for s in range(32):
        to = ((((s >> 3) + z) & 3) << 3) | ((((s >> 1) + x) & 3) << 1) | ((s & 1) ^ c)
        pairs.append((s, to))
    return lax.ppermute(value, "row", pairs)


def shift_x(blocks):
    moved = [blocks[0]]
    for x in range(1, 4):
        moved.append(shift_row(blocks[x], 0, x, 0))
    return moved


def shift_z(blocks):
    moved = [blocks[0]]
    for z in range(1, 4):
        moved.append(shift_row(blocks[z], z, 0, 0))
    return moved


def circuit(amplitudes, gate_matrices, permutation):
    state = amplitudes.reshape(2, 2, 1024, 128)
    mid = ("mid", "mid")
    kinds = (
        ((None, None), mid, ("xor2", None)),
        ((None, "xor2"), mid, (None, None)),
        ((None, None), mid, ("dest", None)),
        ((None, "src"), mid, ("xor4", None)),
        ((None, "xor4"), mid, (None, None)),
    )
    w = [
        weights(gate_matrices, seg, kinds[seg], permutation if seg == 3 else None)
        for seg in range(5)
    ]
    low = low_weights(gate_matrices)
    halves = (0, 1)
    kept, sent, got = {}, {}, {}
    stays, leaves, whole = pack(state)
    firsts = ("start",), [stays, flip(leaves, "row", 16)]
    for h in halves:
        source, ins = firsts if h == 0 else (("whole",), [whole])
        kept[h], out = run_segment(source, "pair", w[0], ins)
        sent[h] = flip(out, "row", 1)
        pair = [kept[h], sent[h]]
        if h == 0:
            pair = run_segment(("pair",), "plain", w[1], pair)
        else:
            stays, leaves = run_segment(("pair",), "leave", w[1], pair)
            pair = [stays, flip(leaves, "row", 16)]
        near, far = run_segment(("turn", "join")[h : h + 1], "remap", w[2], pair)
        pair = [near, flip(far, "row", 1)]
        if h == 0:
            moved = shift_z(regroup("by_z", pair))
            got[h] = shift_x(regroup("swap", moved))
        else:
            moved = shift_x(regroup("by_x", pair))
            got[h] = shift_z(regroup("swap", moved))
    for h in halves:
        kept[h], out = run_segment(("remap", ("by_x", "by_z")[h]), "pair", w[3], got[h])
        sent[h] = flip(out, "col", 4)
    (share,) = run_segment(("pair", 0), "share", w[4], [kept[0], sent[0]], [low], unroll=4)
    (out,) = run_segment(("pair", 1), "low", w[4], [kept[1], sent[1]], [share, low])
    return out.reshape(amplitudes.shape)


def solution(mesh):
    placed = (P(None, "row", "col", None), P(), P())
    return jax.shard_map(
        circuit, mesh=mesh, in_specs=placed, out_specs=P(None, "row", "col", None), check_vma=False
    )
```

```python
import functools

import jax
import jax.numpy as jnp
from jax import lax
from jax.experimental import pallas as pl
from jax.experimental.pallas import tpu as pltpu
from jax.sharding import PartitionSpec as P


F32 = jnp.float32
BF16 = jnp.bfloat16
GD = 128
HALF = 64
LIMIT = 16 << 20
STATE = (16, 16, 8, 128)
PART = (8, 16, 8, 128)


def split(value):
    high = value.astype(BF16)
    return high, (value - high.astype(F32)).astype(BF16)


def onehot(kind, perm_ref):
    row = lax.axis_index("row")
    col = lax.axis_index("col")
    new = lax.broadcasted_iota(jnp.int32, (GD, GD), 0)
    old = lax.broadcasted_iota(jnp.int32, (GD, GD), 1)
    z_own, x_own, c_own = row >> 3, (row >> 1) & 3, row & 1
    rest, core, block = new & 3, (new >> 2) & 1, new >> 3
    if kind == "mid":
        want = ((new & 7) << 4) | (new >> 3)
    elif kind[:3] == "xor":
        want = new ^ ({"xor2": c_own, "xor4": col >> 2}[kind] << 6)
    elif kind == "dest":
        x = ((block >> 2) + x_own) & 3
        z = ((block & 3) + z_own) & 3
        want = (((((z << 2) | x) << 1) | (core ^ c_own)) << 2) | rest
    else:
        z = ((block >> 3) << 1) | ((z_own - (block >> 2)) & 1)
        x = (x_own - (block & 3)) & 3
        want = (((((z << 2) | x) << 1) | (core ^ c_own)) << 2) | rest
        state = lax.broadcasted_iota(jnp.int32, (1, GD), 1)
        moved = state & 3
        for t in range(32):
            moved += jnp.where(state >> 2 == t, perm_ref[t] * 4, 0)
        old = jnp.broadcast_to(moved, (GD, GD))
    return jnp.where(want == old, 1.0, 0.0).astype(BF16)


def weight_kernel(kinds, n_prefetch, *refs):
    perm_ref = refs[0] if n_prefetch else None
    gates_ref, out_ref = refs[n_prefetch], refs[-1]
    made = {}
    for number, (rows, cols) in enumerate(kinds):
        for kind in (rows, cols):
            if kind is not None and kind not in made:
                made[kind] = onehot(kind, perm_ref)
        slot = (0, 1, 3)[number]
        real_high, real_low = split(gates_ref[0, slot, 0])
        imag_high, imag_low = split(gates_ref[0, slot, 1])
        wide = jnp.concatenate([real_high, imag_high, real_low, imag_low], axis=1)
        if rows is not None:
            wide = jnp.dot(made[rows], wide, preferred_element_type=F32).astype(BF16)
        parts = [wide[:, GD * i : GD * (i + 1)] for i in range(4)]
        if cols is not None:
            tall = lax.dot_general(
                jnp.concatenate(parts, axis=0),
                made[cols],
                (((1,), (1,)), ((), ())),
                preferred_element_type=F32,
            ).astype(BF16)
            parts = [tall[GD * i : GD * (i + 1)] for i in range(4)]
        out_ref[number, 0:GD, 0:GD] = parts[0]
        out_ref[number, 0:GD, GD:] = parts[1]
        out_ref[number, GD:, 0:GD] = parts[2]
        out_ref[number, GD:, GD:] = parts[3]


def weights(gate_matrices, seg, kinds, permutation):
    prefetch = () if permutation is None else (permutation,)
    block = seg
    if seg == 0:
        block, gate_matrices = 0, gate_matrices[:1]
    return pl.pallas_call(
        functools.partial(weight_kernel, kinds, len(prefetch)),
        out_shape=jax.ShapeDtypeStruct((3, 256, 256), BF16),
        grid_spec=pltpu.PrefetchScalarGridSpec(
            num_scalar_prefetch=len(prefetch),
            grid=(1,),
            in_specs=[pl.BlockSpec((1, 4, 2, GD, GD), lambda i, *_: (block, 0, 0, 0, 0))],
            out_specs=pl.BlockSpec(memory_space=pltpu.VMEM),
        ),
        cost_estimate=pl.CostEstimate(
            flops=3 * 2 * 640 * 128 * 512, bytes_accessed=1 << 20, transcendentals=0
        ),
        compiler_params=pltpu.CompilerParams(vmem_limit_bytes=LIMIT),
    )(*prefetch, gate_matrices)


def low_kernel(gates_ref, out_ref, total_ref):
    seg = pl.program_id(0)
    real, imag = gates_ref[0, 0, 0], gates_ref[0, 0, 1]
    form = jnp.concatenate(
        [jnp.concatenate([real, -imag], axis=1), jnp.concatenate([imag, real], axis=1)], axis=0
    )

    @pl.when(seg == 0)
    def _():
        new = lax.broadcasted_iota(jnp.int32, (256, 256), 0)
        old = lax.broadcasted_iota(jnp.int32, (256, 256), 1)
        want = (((new >> 6) & 1) << 7) | (((new >> 5) & 1) << 6) | ((new >> 7) << 5) | (new & 31)
        total_ref[...] = jnp.where(want == old, 1.0, 0.0)

    high, low = split(total_ref[...])
    form_high, form_low = split(form)

    def times(left, right):
        return lax.dot_general(
            left, right, (((1,), (1,)), ((), ())), preferred_element_type=F32
        )

    total = times(high, form_high) + (times(high, form_low) + times(low, form_high))
    total_ref[...] = total
    for k, piece in enumerate(split(total)):
        for h in range(2):
            rows = piece[GD * h : GD * (h + 1)]
            out_ref[h, k, 0:GD] = rows
            out_ref[h, k, GD:] = rows


def low_weights(gate_matrices):
    return pl.pallas_call(
        low_kernel,
        out_shape=jax.ShapeDtypeStruct((2, 2, 256, 256), BF16),
        grid=(gate_matrices.shape[0],),
        in_specs=[pl.BlockSpec((1, 1, 2, GD, GD), lambda i: (i, 2, 0, 0, 0))],
        out_specs=pl.BlockSpec(memory_space=pltpu.VMEM),
        scratch_shapes=[pltpu.VMEM((256, 256), F32)],
        cost_estimate=pl.CostEstimate(
            flops=5 * 3 * 2 * 256**3, bytes_accessed=1 << 20, transcendentals=0
        ),
        compiler_params=pltpu.CompilerParams(vmem_limit_bytes=LIMIT),
        name="low_weights",
    )(gate_matrices)


def cross(first, second, step):
    axis = first.ndim - 1
    lane = lax.broadcasted_iota(jnp.int32, (1,) * axis + (GD,), axis)
    off = (lane & step) == 0
    return (
        jnp.where(off, first, pltpu.roll(second, step, axis)),
        jnp.where(off, pltpu.roll(first, GD - step, axis), second),
    )


def in_order(swapped, first, second):
    return jnp.where(swapped, second, first), jnp.where(swapped, first, second)


def turned(blocks):
    sub = lax.broadcasted_iota(jnp.int32, (1, 8, 1), 1)
    for step in (1, 2, 4):
        off = (sub & step) == 0
        made = [None] * 8
        for k in range(8):
            if k & step:
                continue
            first, second = blocks[k], blocks[k + step]
            made[k] = jnp.where(off, first, pltpu.roll(second, step, 1))
            made[k + step] = jnp.where(off, pltpu.roll(first, 8 - step, 1), second)
        blocks = made
    return blocks


def pack_kernel(state_ref, *outs):
    own = lax.axis_index("row") >> 4 == 1

    tops = [cross(state_ref[0, t], state_ref[1, t], 64) for t in range(2)]
    sides = [cross(tops[0][b], tops[1][b], 32)[0] for b in range(2)]
    for out, side in zip(outs[:2], in_order(own, *sides)):
        out[...] = side
    for t in range(2):
        outs[2][t] = cross(*tops[t], 32)[1]


def pack(state):
    part = pl.BlockSpec((256, GD), lambda i: (i, 0))
    return pl.pallas_call(
        pack_kernel,
        out_shape=[
            jax.ShapeDtypeStruct(shape, F32)
            for shape in ((1024, 128), (1024, 128), (2, 1024, 128))
        ],
        grid=(4,),
        in_specs=[pl.BlockSpec((2, 2, 256, GD), lambda i: (0, 0, i, 0))],
        out_specs=[part, part, pl.BlockSpec((2, 256, GD), lambda i: (0, i, 0))],
        cost_estimate=pl.CostEstimate(flops=0, bytes_accessed=4 << 20, transcendentals=0),
        compiler_params=pltpu.CompilerParams(vmem_limit_bytes=60 << 20),
        name="pack",
    )(state)


def gate_step(first, second, w_high_low, w_high, sign):
    state = jnp.concatenate([first, second], axis=1)
    turned = jnp.concatenate(
        [pltpu.roll(first, HALF, 1) * sign, pltpu.roll(second, HALF, 1) * sign], axis=1
    )
    high, low = split(jnp.concatenate([state, turned], axis=0))
    both = jnp.dot(w_high_low, high, preferred_element_type=F32)
    small = jnp.dot(w_high, low, preferred_element_type=F32)
    return both[:GD] + (both[GD:] + small)


def segment_kernel(source, target, n_in, unroll, *refs):
    w_ref = refs[0]
    ins = refs[1 : 1 + n_in]
    outs = refs[1 + n_in : -2]
    one, two = refs[-2:]
    lane = lax.broadcasted_iota(jnp.int32, (1, GD), 1)
    sign = jnp.where(lane < HALF, -1.0, 1.0)
    upper = lax.broadcasted_iota(jnp.int32, (1, 8, GD), 1) >= 4

    own = lax.axis_index("row") >> 4 == 1

    def load_start(i):
        blocks = []
        for p in (2 * i, 2 * i + 1):
            rows = pl.ds(p, HALF, stride=16)
            sides = in_order(own, ins[0][rows, :], ins[1][rows, :])
            blocks.append(jnp.concatenate(cross(*sides, 32), axis=0))
        return blocks

    def load_whole(i):
        blocks = []
        for p in (2 * i, 2 * i + 1):
            rows = pl.ds(p, HALF, stride=16)
            blocks.append(jnp.concatenate([ins[0][0, rows, :], ins[0][1, rows, :]], axis=0))
        return blocks

    def load_join(i):
        blocks = []
        for p in (2 * i, 2 * i + 1):
            sides = in_order(own, ins[0][:, p].reshape(HALF, GD), ins[1][:, p].reshape(HALF, GD))
            blocks.append(jnp.concatenate(sides, axis=0))
        return blocks

    def load_turn(i):
        blocks = []
        for p in (2 * i, 2 * i + 1):
            sides = ins[0][:8, p].reshape(HALF, GD), ins[0][8:, p].reshape(HALF, GD)
            blocks.append(jnp.concatenate(cross(*sides, 32), axis=0))
        return blocks

    def load_pair(i):
        return [
            jnp.concatenate(
                [ins[0][:, p].reshape(HALF, GD), ins[1][:, p].reshape(HALF, GD)], axis=0
            )
            for p in (2 * i, 2 * i + 1)
        ]

    def load_remap(i):
        def half(c):
            if source[1] == "by_x":
                return jnp.stack([ins[x][c, z, i] for z in range(4) for x in range(4)], axis=0)
            return jnp.concatenate([ins[z][c, :, i] for z in range(4)], axis=0)

        near, far = half(0), half(1)
        even = jnp.where(upper, pltpu.roll(far, 4, 1), near)
        odd = jnp.where(upper, far, pltpu.roll(near, 4, 1))
        z_own = lax.axis_index("row") >> 3
        blocks = []
        for rows in (even, odd):
            near_rows = [], []
            for z in range(2):
                swapped = ((z_own - z) & 3) >= 2
                sides = in_order(swapped, rows[4 * z : 4 * z + 4], rows[4 * z + 8 : 4 * z + 12])
                for k, side in enumerate(cross(*sides, 32)):
                    near_rows[k].append(side)
            blocks.append(jnp.concatenate(near_rows[0] + near_rows[1], axis=0).reshape(GD, GD))
        return blocks

    load = {
        "start": load_start,
        "pair": load_pair,
        "turn": load_turn,
        "whole": load_whole,
        "join": load_join,
        "remap": load_remap,
    }[source[0]]

    def top_first(i, carry):
        first, second = load(i)
        result = gate_step(first, second, w_ref[0], w_ref[0, :GD], sign)
        one[:, 2 * i] = result[:, :GD].reshape(16, 8, GD)
        one[:, 2 * i + 1] = result[:, GD:].reshape(16, 8, GD)
        return carry

    def mid(i, carry):
        first = one[2 * i].reshape(GD, GD)
        second = one[2 * i + 1].reshape(GD, GD)
        result = gate_step(first, second, w_ref[1], w_ref[1, :GD], sign)
        two[2 * i] = result[:, :GD].reshape(16, 8, GD)
        two[2 * i + 1] = result[:, GD:].reshape(16, 8, GD)
        return carry

    def top_last(i, carry):
        first = two[:, 2 * i].reshape(GD, GD)
        second = two[:, 2 * i + 1].reshape(GD, GD)
        result = gate_step(first, second, w_ref[2], w_ref[2, :GD], sign)
        pieces = (result[:, :GD], result[:, GD:])
        if target == "pair":
            for p, piece in zip((2 * i, 2 * i + 1), pieces):
                outs[0][:, p] = piece[:HALF].reshape(8, 8, GD)
                outs[1][:, p] = piece[HALF:].reshape(8, 8, GD)
        elif target == "leave":
            for p, piece in zip((2 * i, 2 * i + 1), pieces):
                sides = in_order(own, *cross(piece[:HALF], piece[HALF:], 32))
                for out, side in zip(outs, sides):
                    out[:, p] = side.reshape(8, 8, GD)
        elif target == "remap":
            even, odd = (piece.reshape(16, 8, GD) for piece in pieces)
            outs[0][:, i] = jnp.where(upper, pltpu.roll(odd, 4, 1), even)
            outs[1][:, i] = jnp.where(upper, odd, pltpu.roll(even, 4, 1))
        else:
            held = outs[0] if target == "plain" else one
            for p, piece in zip((2 * i, 2 * i + 1), pieces):
                held[:, p] = piece.reshape(16, 8, GD)
        return carry

    def low_gate(i, carry):
        low_ref = ins[-1]
        rows = one[pl.ds(4 * i, 4)].reshape(512, GD)
        pair = jnp.concatenate(split(rows), axis=1)
        done = jnp.dot(pair, low_ref[source[1], 0], preferred_element_type=F32) + jnp.dot(
            pair, low_ref[source[1], 1], preferred_element_type=F32
        )
        if target == "share":
            outs[0][i] = done
            return carry
        done = done + ins[-2][i]
        for c in range(2):
            part = done[:, GD * c : GD * (c + 1)].reshape(4, 2, 8, 8, GD)
            blocks = [part[:, :, k].reshape(8, 8, GD) for k in range(8)]
            for o, block in enumerate(turned(blocks)):
                outs[0][c, pl.ds(4 * i, 4), o] = block.reshape(4, 2, 8, GD)
        return carry

    for step in (top_first, mid, top_last):
        lax.fori_loop(0, 8, step, 0, unroll=unroll)
    if target in ("share", "low"):
        lax.fori_loop(0, 4, low_gate, 0, unroll=4 if unroll == 8 else 1)


def run_segment(source, target, w, ins, extra=(), unroll=8):
    if target in ("pair", "leave"):
        out_shape = [jax.ShapeDtypeStruct(PART, F32)] * 2
    elif target == "remap":
        out_shape = [jax.ShapeDtypeStruct((16, 8, 8, 128), F32)] * 2
    elif target == "plain":
        out_shape = [jax.ShapeDtypeStruct(STATE, F32)]
    elif target == "share":
        out_shape = [jax.ShapeDtypeStruct((4, 512, 256), F32)]
    else:
        out_shape = [jax.ShapeDtypeStruct((2, 16, 8, 2, 8, 128), F32)]
    args = list(ins) + list(extra)
    vmem = pl.BlockSpec(memory_space=pltpu.VMEM)
    return pl.pallas_call(
        functools.partial(segment_kernel, source, target, len(args), unroll),
        out_shape=out_shape,
        in_specs=[vmem] * (1 + len(args)),
        out_specs=[vmem] * len(out_shape),
        scratch_shapes=[pltpu.VMEM(STATE, F32)] * 2,
        cost_estimate=pl.CostEstimate(
            flops=3 * 3 * 2 * 128 * 256 * 2048, bytes_accessed=3 << 20, transcendentals=0
        ),
        compiler_params=pltpu.CompilerParams(vmem_limit_bytes=LIMIT),
    )(w, *args)


def regroup_kernel(order, *refs):
    ins, outs = refs[:-4], refs[-4:]
    for j in range(4):
        for k in range(4):
            for c in range(2):
                if order == "swap":
                    outs[j][c, k] = ins[k][c, j]
                else:
                    outs[j][c, k] = ins[c][4 * j + k if order == "by_x" else 4 * k + j]


def regroup(order, blocks):
    vmem = pl.BlockSpec(memory_space=pltpu.VMEM)
    return pl.pallas_call(
        functools.partial(regroup_kernel, order),
        out_shape=[jax.ShapeDtypeStruct((2, 4, 8, 8, 128), F32)] * 4,
        in_specs=[vmem] * len(blocks),
        out_specs=[vmem] * 4,
        cost_estimate=pl.CostEstimate(flops=0, bytes_accessed=2 << 20, transcendentals=0),
        compiler_params=pltpu.CompilerParams(vmem_limit_bytes=LIMIT),
    )(*blocks)


def flip(value, axis, mask):
    return lax.ppermute(value, axis, [(s, s ^ mask) for s in range(lax.axis_size(axis))])


def shift_row(value, z, x, c):
    pairs = []
    for s in range(32):
        to = ((((s >> 3) + z) & 3) << 3) | ((((s >> 1) + x) & 3) << 1) | ((s & 1) ^ c)
        pairs.append((s, to))
    return lax.ppermute(value, "row", pairs)


def shift_x(blocks):
    moved = [blocks[0]]
    for x in range(1, 4):
        moved.append(shift_row(blocks[x], 0, x, 0))
    return moved


def shift_z(blocks):
    moved = [blocks[0]]
    for z in range(1, 4):
        moved.append(shift_row(blocks[z], z, 0, 0))
    return moved


def circuit(amplitudes, gate_matrices, permutation):
    state = amplitudes.reshape(2, 2, 1024, 128)
    mid = ("mid", "mid")
    kinds = (
        ((None, None), mid, ("xor2", None)),
        ((None, "xor2"), mid, (None, None)),
        ((None, None), mid, ("dest", None)),
        ((None, "src"), mid, ("xor4", None)),
        ((None, "xor4"), mid, (None, None)),
    )
    w = [
        weights(gate_matrices, seg, kinds[seg], permutation if seg == 3 else None)
        for seg in range(5)
    ]
    low = low_weights(gate_matrices)
    halves = (0, 1)
    kept, sent, got = {}, {}, {}
    stays, leaves, whole = pack(state)
    firsts = ("start",), [stays, flip(leaves, "row", 16)]
    for h in halves:
        source, ins = firsts if h == 0 else (("whole",), [whole])
        kept[h], out = run_segment(source, "pair", w[0], ins)
        sent[h] = flip(out, "row", 1)
        pair = [kept[h], sent[h]]
        if h == 0:
            pair = run_segment(("pair",), "plain", w[1], pair)
        else:
            stays, leaves = run_segment(("pair",), "leave", w[1], pair)
            pair = [stays, flip(leaves, "row", 16)]
        near, far = run_segment(("turn", "join")[h : h + 1], "remap", w[2], pair)
        pair = [near, flip(far, "row", 1)]
        if h == 0:
            moved = shift_z(regroup("by_z", pair))
            got[h] = shift_x(regroup("swap", moved))
        else:
            moved = shift_x(regroup("by_x", pair))
            got[h] = shift_z(regroup("swap", moved))
    for h in halves:
        kept[h], out = run_segment(("remap", ("by_x", "by_z")[h]), "pair", w[3], got[h])
        sent[h] = flip(out, "col", 4)
    (share,) = run_segment(("pair", 0), "share", w[4], [kept[0], sent[0]], [low], unroll=4)
    (out,) = run_segment(("pair", 1), "low", w[4], [kept[1], sent[1]], [share, low])
    return out.reshape(amplitudes.shape)


def solution(mesh):
    placed = (P(None, "row", "col", None), P(), P())
    return jax.shard_map(
        circuit, mesh=mesh, in_specs=placed, out_specs=P(None, "row", "col", None), check_vma=False
    )
```
